512 devices in a mesh: cells: 32 (over y, x), genes: 16 (over z, core).
Axes of the slice: x: 4, y: 8, z: 8, core: 2. Of those that a mesh axis runs over, the one named last changes fastest.
Arguments:
- counts: int32 [32768, 4096], P('cells', 'genes'), may hold values from 0 to 128, as said below
- batch: int32 [32768, 1], P(('cells', 'genes')), may hold values from 0 to 63
- seeds: int32 [32768, 1], P(('cells', 'genes')), may hold values from 0 to 1023
- loadings: bfloat16 [4096, 256], P('genes'), may hold values from -0.09375 to 0.09375
Outputs:
- embedding: float32 [32768, 256], P(('cells', 'genes'))
- assign: float32 [32768, 1024], P(('cells', 'genes'))
- centroids: bfloat16 [1024, 256], replicated
The draws below stay inside these ranges and needn't reach their ends.
Inputs may be any that keep to these rules, and one draw needn't show every extreme that they name: counts[i, g] >= 1 wherever g mod 64 equals i mod 64. `batch`: every label occurs. `seeds`: every cluster is the seed of some cell.
All inputs are finite; a program needn't handle non-finite values.
Results may differ from the reference program's by a relative error of at most 0.012.
The reference program's roundings to bfloat16 on the way (of `logged` and `unit_rows`) count: a program that leaves them out, or rounds other values in their place, can miss the bound.
Values may be sent and summed in bfloat16 or wider, within the bound.
No kernel may reach another device: no remote copies, remote signals or barrier semaphores. Data moves between devices by JAX's collectives and lax.ppermute only.
A program may use at most 64 MiB of HBM per device.

```python
from functools import partial
import jax
import jax.numpy as jnp
from jax import lax

G = 4096
D = 256
K = 1024
B = 64
ITERS = 2
CELLS = 32768
N_CELLS = 32


def draw_counts(key, part):
    level_key, depth_key, value_key, retain_key = jax.random.split(key, 4)
    gene_index = jnp.arange(G, dtype=jnp.int32)
    gene_level = 3 + gene_index * 12 // G + jax.random.randint(level_key, (G,), 0, 3, dtype=jnp.int32)
    cell_depth = jax.random.randint(depth_key, (CELLS, 1), 1, 9, dtype=jnp.int32)
    limits = gene_level[None, :] * cell_depth + 1
    values = jax.random.randint(value_key, (CELLS, G), 0, limits, dtype=jnp.int32)
    retained = jax.random.randint(retain_key, (CELLS, G), 0, 3, dtype=jnp.int32) > 0
    cell_index = jnp.arange(CELLS, dtype=jnp.int32)[:, None]
    diagonal_one = (gene_index[None, :] % 64 == cell_index % 64).astype(jnp.int32)
    return jnp.maximum(jnp.where(retained, values, 0), diagonal_one)


def steps_of(key, shape, cuts, least, largest):
    factor_of = 1.0
    for axis_at, blocks in cuts:
        steps = jax.random.uniform(jax.random.fold_in(jax.random.fold_in(key, 6), axis_at), (blocks,), jnp.float32, least / len(cuts), largest / len(cuts))
        factor_of = factor_of * jnp.repeat(jnp.exp(steps), shape[axis_at] // blocks).reshape((-1,) + (1,) * (len(shape) - 1 - axis_at))
    return factor_of


def different_ones(stream_key, rows, amount, top, lift):
    ranking = jax.random.permutation(jax.random.fold_in(stream_key, 1), amount)
    pull = ranking
    for power in range(3):
        pull = pull * pull // amount
    pull = pull * lift // amount
    tickets = jax.random.randint(jax.random.fold_in(stream_key, 2), (rows, amount), 0, 4096) + pull
    sure = jax.random.permutation(jax.random.fold_in(stream_key, 3), rows)[jnp.arange(amount) % rows]
    tickets = jnp.where(jnp.arange(rows)[:, None] == sure[None, :], 1 << 14, tickets)
    priority = tickets * amount + jnp.arange(amount)
    return lax.top_k(priority.astype(jnp.int32), top)[1].astype(jnp.int32)


def scatter_about(own_key, extent, spread, reach, shards=(), held_as=jnp.bfloat16):
    result = spread * jax.random.normal(own_key, extent, jnp.float32)
    if shards:
        result = result * steps_of(own_key, extent, shards, -0.22, 0.18)
    return jnp.clip(result, -reach, reach).astype(held_as)


def setup_inputs(seed: int = 0) -> dict:
    splits = jax.random.split(jax.random.key(seed), 5)
    return {
        "counts": draw_counts(jax.random.fold_in(splits[4], 71), 0),
        "batch": different_ones(splits[1], CELLS, B, 1, 128),
        "seeds": different_ones(splits[2], CELLS, K, 1, 0),
        "loadings": scatter_about(splits[3], (G, D), G ** -0.5, 0.09375, ((0, 16),)),
    }


epsilon = 1e-06
cluster_spread = 0.1

def project_block(block, loadings):
    values = block.astype(jnp.float32)
    depth_total = lax.optimization_barrier(jnp.sum(values, axis=1, keepdims=True))
    logged = jnp.log1p(10000.0 * values / depth_total).astype(jnp.bfloat16)
    return jnp.dot(logged, loadings, preferred_element_type=jnp.float32)

def cluster_tables(cluster_sums, observed, batch_total, total_cells):
    scaled = cluster_sums * lax.rsqrt(lax.optimization_barrier(jnp.sum(cluster_sums * cluster_sums, axis=1, keepdims=True)) + epsilon)
    cluster_mass = lax.optimization_barrier(jnp.sum(observed, axis=1, keepdims=True))
    expected = cluster_mass * batch_total[None, :] / total_cells
    ratio = (expected + 1.0) / (observed + 1.0)
    return (scaled.astype(jnp.bfloat16), ratio * ratio)

def reference(counts, batch, seeds, loadings):
    blocks = counts.reshape(N_CELLS, CELLS // N_CELLS, G)
    projected = lax.map(partial(project_block, loadings=loadings), blocks).reshape(CELLS, D)
    center = lax.optimization_barrier(jnp.sum(projected, axis=0)) / CELLS
    embedding = projected - center
    unit_rows = (embedding * lax.rsqrt(lax.optimization_barrier(jnp.sum(embedding * embedding, axis=1, keepdims=True)) + epsilon)).astype(jnp.bfloat16)
    labels = batch[:, 0]
    batch_onehot = (batch == jnp.arange(B, dtype=jnp.int32)[None, :]).astype(jnp.float32)
    batch_total = lax.optimization_barrier(jnp.sum(batch_onehot, axis=0))
    assign = (seeds == jnp.arange(K, dtype=jnp.int32)[None, :]).astype(jnp.float32)
    centroids = jnp.zeros((K, D), jnp.bfloat16)
    for iteration in range(ITERS):
        rounded = assign.astype(jnp.bfloat16)
        cluster_sums = jnp.dot(rounded.T, unit_rows, preferred_element_type=jnp.float32)
        observed = jnp.dot(rounded.T, batch_onehot.astype(jnp.bfloat16), preferred_element_type=jnp.float32)
        centroids, penalty = cluster_tables(cluster_sums, observed, batch_total, CELLS)
        distance = 2.0 - 2.0 * jnp.dot(unit_rows, centroids.T, preferred_element_type=jnp.float32)
        weights = jnp.exp(-distance / cluster_spread) * penalty.T[labels]
        assign = weights / lax.optimization_barrier(jnp.sum(weights, axis=1, keepdims=True))
    return (embedding, assign, centroids)
```

```python
import jax
import jax.numpy as jnp
from jax import lax
from jax.sharding import PartitionSpec as P

K = 1024
B = 64
ITERS = 2
CELL_AXIS = "cells"
GENE_AXIS = "genes"

epsilon = 1e-06
cluster_spread = 0.1

f32 = jnp.float32
bf16 = jnp.bfloat16
leading = (((0,), (0,)), ((), ()))
trailing = (((1,), (1,)), ((), ()))


def exchange(blocks, axis):
    return lax.all_to_all(blocks, axis, 0, 0, tiled=False)


def share(block, axis):
    return exchange(jnp.broadcast_to(block[None], (lax.axis_size(axis),) + block.shape), axis)


def one_hot(labels, first, count, dtype):
    return (labels == first + jnp.arange(count, dtype=jnp.int32)[None, :]).astype(dtype)


def halves(value):
    high = value.astype(bf16)
    return high, (value - high.astype(f32)).astype(bf16)


def cluster_rows(sums, observed, batch_total, total_cells):
    scaled = sums * lax.rsqrt(jnp.sum(sums * sums, axis=1, keepdims=True) + epsilon)
    mass = jnp.sum(observed, axis=1, keepdims=True)
    ratio = (mass * batch_total / total_cells + 1.0) / (observed + 1.0)
    high, low = halves(ratio * ratio)
    return jnp.concatenate([scaled.astype(bf16), high, low], axis=1)


def cluster_weights(unit_rows, batch_twice, rows):
    depth = unit_rows.shape[1]
    similarity = lax.dot_general(unit_rows, rows[:, :depth], trailing, preferred_element_type=f32)
    lookup = lax.dot_general(batch_twice, rows[:, depth:], trailing, preferred_element_type=f32)
    distance = 2.0 - 2.0 * similarity
    return jnp.exp(-distance / cluster_spread) * lookup


def per_device(counts, batch, seeds, loadings):
    n_cells, n_genes = lax.axis_size(CELL_AXIS), lax.axis_size(GENE_AXIS)
    group, own = counts.shape[0], batch.shape[0]
    total_cells = group * n_cells
    width = loadings.shape[1]
    mine = K // n_genes
    piece = mine // n_cells

    values = counts.astype(f32)
    packet = jnp.concatenate(
        [jnp.sum(values, axis=1), batch[:, 0].astype(f32), seeds[:, 0].astype(f32)]
    )
    packets = share(packet, GENE_AXIS)
    depth_total = jnp.sum(packets[:, :group], axis=0)
    group_batch = packets[:, group : group + own].reshape(group, 1).astype(jnp.int32)
    group_seeds = packets[:, group + own :].reshape(group, 1).astype(jnp.int32)

    logged = jnp.log1p(10000.0 * values / depth_total[:, None]).astype(bf16)
    partial = jnp.dot(logged, loadings, preferred_element_type=f32)

    batch_hot = one_hot(group_batch, 0, B, bf16)
    first = lax.axis_index(GENE_AXIS) * mine
    assign = one_hot(group_seeds, first, mine, bf16)
    first_observed = lax.dot_general(assign, batch_hot, leading, preferred_element_type=f32)
    group_labels = jnp.sum(batch_hot.astype(f32), axis=0)

    everyone = jnp.concatenate([jnp.sum(partial, axis=0), group_labels])
    packet = jnp.concatenate(
        [
            jnp.broadcast_to(everyone[None], (n_cells, width + B)),
            first_observed.reshape(n_cells, piece * B),
        ],
        axis=1,
    )
    arrived = jnp.sum(exchange(packet, CELL_AXIS), axis=0)
    center = arrived[:width] / total_cells
    batch_total = arrived[width : width + B][None]
    observed = arrived[width + B :].reshape(piece, B)

    centred = (partial - center[None]).astype(bf16).reshape(n_genes, own, width)
    embedding = jnp.sum(exchange(centred, GENE_AXIS).astype(f32), axis=0)
    own_rows = (
        embedding * lax.rsqrt(jnp.sum(embedding * embedding, axis=1, keepdims=True) + epsilon)
    ).astype(bf16)
    unit_rows = share(own_rows, GENE_AXIS).reshape(group, width)

    batch_twice = jnp.concatenate([batch_hot, batch_hot], axis=1)
    for iteration in range(ITERS):
        if iteration == 0:
            sums = lax.dot_general(assign, unit_rows, leading, preferred_element_type=f32)
            sums = jnp.sum(exchange(sums.reshape(n_cells, piece, width), CELL_AXIS), axis=0)
        else:
            weights = cluster_weights(unit_rows, batch_twice, rows)
            norm = jnp.sum(share(jnp.sum(weights, axis=1), GENE_AXIS), axis=0)
            rounded = (weights / norm[:, None]).astype(bf16)
            both = jnp.concatenate([unit_rows, batch_hot], axis=1)
            sums = lax.dot_general(rounded, both, leading, preferred_element_type=f32)
            sums = jnp.sum(exchange(sums.reshape(n_cells, piece, width + B), CELL_AXIS), axis=0)
            sums, observed = sums[:, :width], sums[:, width:]
        rows = cluster_rows(sums, observed, batch_total, total_cells)
        rows = share(rows, CELL_AXIS).reshape(mine, width + 2 * B)

    rows = share(rows, GENE_AXIS).reshape(K, width + 2 * B)
    own_hot = one_hot(batch, 0, B, bf16)
    weights = cluster_weights(own_rows, jnp.concatenate([own_hot, own_hot], axis=1), rows)
    assign = weights / jnp.sum(weights, axis=1, keepdims=True)
    return (embedding, assign, rows[:, :width])


def solution(mesh):
    placed = (
        P("cells", "genes"),
        P(("cells", "genes"), None),
        P(("cells", "genes"), None),
        P("genes", None),
    )
    return jax.shard_map(
        per_device,
        mesh=mesh,
        in_specs=placed,
        out_specs=(P(("cells", "genes"), None), P(("cells", "genes"), None), P()),
        check_vma=False,
    )
```

```python
import jax
import jax.numpy as jnp
from jax import lax
from jax.sharding import PartitionSpec as P

K = 1024
B = 64
ITERS = 2
CELL_AXIS = "cells"
GENE_AXIS = "genes"

epsilon = 1e-06
cluster_spread = 0.1

f32 = jnp.float32
bf16 = jnp.bfloat16
leading = (((0,), (0,)), ((), ()))
trailing = (((1,), (1,)), ((), ()))


def exchange(blocks, axis):
    return lax.all_to_all(blocks, axis, 0, 0, tiled=False)


def share(block, axis):
    return exchange(jnp.broadcast_to(block[None], (lax.axis_size(axis),) + block.shape), axis)


def gather(block, axis):
    return lax.all_gather(block, axis, tiled=True)


def one_hot(labels, count, dtype):
    return (labels == jnp.arange(count, dtype=jnp.int32)[None, :]).astype(dtype)


together = lax.optimization_barrier


def halves(value):
    high = value.astype(bf16)
    return high, (value - high.astype(f32)).astype(bf16)


def unit_centroids(sums):
    scaled = sums * lax.rsqrt(jnp.sum(sums * sums, axis=1, keepdims=True) + epsilon)
    return scaled.astype(bf16)


def penalty_halves(observed, batch_total, total_cells):
    mass = jnp.sum(observed, axis=1, keepdims=True)
    ratio = (mass * batch_total / total_cells + 1.0) / (observed + 1.0)
    return jnp.concatenate(halves(ratio * ratio), axis=1)


def cluster_weights(unit_rows, batch_twice, rows):
    depth = unit_rows.shape[1]
    similarity = lax.dot_general(unit_rows, rows[:, :depth], trailing, preferred_element_type=f32)
    lookup = lax.dot_general(batch_twice, rows[:, depth:], trailing, preferred_element_type=f32)
    distance = 2.0 - 2.0 * similarity
    return jnp.exp(-distance / cluster_spread) * lookup


def per_device(counts, batch, seeds, loadings):
    n_cells, n_genes = lax.axis_size(CELL_AXIS), lax.axis_size(GENE_AXIS)
    group, own = counts.shape[0], batch.shape[0]
    total_cells = group * n_cells
    width = loadings.shape[1]
    mine = K // n_genes
    piece = mine // n_cells

    values = counts.astype(f32)
    packet = jnp.concatenate(
        [jnp.sum(values, axis=1), batch[:, 0].astype(f32), seeds[:, 0].astype(f32)]
    )
    own_hot = one_hot(batch, B, bf16)
    first = lax.axis_index(GENE_AXIS) * mine
    packet, own_twice, first = together(
        (packet, jnp.concatenate([own_hot, own_hot], axis=1), first)
    )
    packets = share(packet, GENE_AXIS)
    depth_total = jnp.sum(packets[:, :group], axis=0)
    group_batch = packets[:, group : group + own].reshape(group, 1).astype(jnp.int32)
    group_seeds = packets[:, group + own :].reshape(group, 1).astype(jnp.int32)

    logged = jnp.log1p(10000.0 * values / depth_total[:, None]).astype(bf16)
    partial = jnp.dot(logged, loadings, preferred_element_type=f32)

    batch_hot = one_hot(group_batch, B, bf16)
    assign = one_hot(group_seeds - first, mine, bf16)
    first_observed = lax.dot_general(assign, batch_hot, leading, preferred_element_type=f32)
    group_labels = jnp.sum(batch_hot.astype(f32), axis=0)

    everyone = jnp.concatenate([jnp.sum(partial, axis=0), group_labels])
    packet = jnp.concatenate(
        [
            jnp.broadcast_to(everyone[None], (n_cells, width + B)),
            first_observed.reshape(n_cells, piece * B),
        ],
        axis=1,
    )
    batch_twice = jnp.concatenate([batch_hot, batch_hot], axis=1)
    packet, batch_hot, batch_twice, assign = together((packet, batch_hot, batch_twice, assign))
    arrived = jnp.sum(exchange(packet, CELL_AXIS), axis=0)
    center = arrived[:width] / total_cells
    batch_total = arrived[width : width + B][None]
    observed = arrived[width + B :].reshape(piece, B)
    penalty = penalty_halves(observed, batch_total, total_cells)

    centred = (partial - center[None]).astype(bf16).reshape(n_genes, own, width)
    centred, penalty, batch_total = together((centred, penalty, batch_total))
    embedding = jnp.sum(exchange(centred, GENE_AXIS).astype(f32), axis=0)
    own_rows = (
        embedding * lax.rsqrt(jnp.sum(embedding * embedding, axis=1, keepdims=True) + epsilon)
    ).astype(bf16)
    unit_rows = gather(own_rows, GENE_AXIS)

    for iteration in range(ITERS):
        if iteration == 0:
            sums = lax.dot_general(assign, unit_rows, leading, preferred_element_type=f32)
            sums = jnp.sum(exchange(sums.reshape(n_cells, piece, width), CELL_AXIS), axis=0)
        else:
            weights = cluster_weights(unit_rows, batch_twice, rows)
            norm = jnp.sum(share(jnp.sum(weights, axis=1), GENE_AXIS), axis=0)
            rounded = (weights / norm[:, None]).astype(bf16)
            both = jnp.concatenate([unit_rows, batch_hot], axis=1)
            sums = lax.dot_general(rounded, both, leading, preferred_element_type=f32)
            sums = jnp.sum(exchange(sums.reshape(n_cells, piece, width + B), CELL_AXIS), axis=0)
            penalty = penalty_halves(sums[:, width:], batch_total, total_cells)
            sums = sums[:, :width]
        rows = jnp.concatenate([unit_centroids(sums), penalty], axis=1)
        rows = share(rows, CELL_AXIS).reshape(mine, width + 2 * B)

    rows = gather(rows, GENE_AXIS)
    weights = cluster_weights(own_rows, own_twice, rows)
    assign = weights / jnp.sum(weights, axis=1, keepdims=True)
    return (embedding, assign, rows[:, :width])


def solution(mesh):
    placed = (
        P("cells", "genes"),
        P(("cells", "genes"), None),
        P(("cells", "genes"), None),
        P("genes", None),
    )
    return jax.shard_map(
        per_device,
        mesh=mesh,
        in_specs=placed,
        out_specs=(P(("cells", "genes"), None), P(("cells", "genes"), None), P()),
        check_vma=False,
    )
```

```python
import jax
import jax.numpy as jnp
from jax import lax
from jax.sharding import PartitionSpec as P

K = 1024
B = 64
ITERS = 2
CELL_AXIS = "cells"
GENE_AXIS = "genes"

epsilon = 1e-06
cluster_spread = 0.1

f32 = jnp.float32
bf16 = jnp.bfloat16
trailing = (((1,), (1,)), ((), ()))
together = lax.optimization_barrier


def exchange(blocks, axis):
    return lax.all_to_all(blocks, axis, 0, 0, tiled=False)


def share(block, axis):
    return exchange(jnp.broadcast_to(block[None], (lax.axis_size(axis),) + block.shape), axis)


def gather(block, axis):
    return lax.all_gather(block, axis, tiled=True)


def dot(left, right):
    return jnp.dot(left, right, preferred_element_type=f32)


def dot_rows(left, right):
    return lax.dot_general(left, right, trailing, preferred_element_type=f32)


def hot_columns(labels, count):
    return (labels[None, :] == jnp.arange(count, dtype=f32)[:, None]).astype(bf16)


def halves(value):
    high = value.astype(bf16)
    return high, (value - high.astype(f32)).astype(bf16)


def unit(rows):
    scaled = rows * lax.rsqrt(jnp.sum(rows * rows, axis=1, keepdims=True) + epsilon)
    return scaled.astype(bf16)


def penalty_halves(observed, batch_total, total_cells):
    mass = jnp.sum(observed, axis=1, keepdims=True)
    ratio = (mass * batch_total / total_cells + 1.0) / (observed + 1.0)
    return jnp.concatenate(halves(ratio * ratio), axis=1)


def weigh(similarity, lookup):
    distance = 2.0 - 2.0 * similarity
    return jnp.exp(-distance / cluster_spread) * lookup


def per_device(counts, batch, seeds, loadings):
    n_cells, n_genes = lax.axis_size(CELL_AXIS), lax.axis_size(GENE_AXIS)
    group, own = counts.shape[0], batch.shape[0]
    total_cells = group * n_cells
    width = loadings.shape[1]
    mine = K // n_genes
    piece = mine // n_cells

    values = counts.astype(f32)
    own_hot = (batch == jnp.arange(B, dtype=jnp.int32)[None, :]).astype(f32)
    own_twice = jnp.concatenate([own_hot, own_hot], axis=1).astype(bf16)
    first = (lax.axis_index(GENE_AXIS) * mine).astype(f32)
    packet = jnp.concatenate(
        [
            jnp.sum(values, axis=1),
            batch[:, 0].astype(f32),
            seeds[:, 0].astype(f32),
            jnp.sum(own_hot, axis=0),
        ]
    )
    packet, own_twice, first = together((packet, own_twice, first))
    packets = share(packet, GENE_AXIS)
    depth_total = jnp.sum(packets[:, :group], axis=0)
    at = group
    group_batch = packets[:, at : at + own].reshape(group)
    group_seeds = packets[:, at + own : at + 2 * own].reshape(group)
    group_labels = jnp.sum(packets[:, at + 2 * own :], axis=0)

    logged = jnp.log1p(10000.0 * values / depth_total[:, None]).astype(bf16)
    partial = dot(logged, loadings)

    batch_hot = hot_columns(group_batch, B)
    assign = hot_columns(group_seeds - first, mine)
    first_observed = dot_rows(assign, batch_hot)

    block_mean = jnp.sum(partial, axis=0) / group
    high, low = halves(block_mean[None])
    beside = jnp.concatenate([high] * 4 + [low] * 4, axis=0)
    spread = jnp.concatenate(
        [
            (partial - block_mean[None]).astype(bf16).reshape(n_genes, own, width),
            jnp.broadcast_to(beside[None], (n_genes, 8, width)),
        ],
        axis=1,
    )
    batch_twice = jnp.concatenate([batch_hot, batch_hot], axis=0)
    first_observed = first_observed.reshape(n_cells, piece * B)
    spread, batch_hot, batch_twice, assign, first_observed = together(
        (spread, batch_hot, batch_twice, assign, first_observed)
    )
    shares = exchange(spread, GENE_AXIS).astype(f32)
    about = jnp.sum(shares[:, :own], axis=0)
    group_mean = jnp.sum(shares[:, own] + shares[:, own + 4], axis=0)

    everyone = jnp.concatenate([group_mean, group_labels])
    packet = jnp.concatenate(
        [
            jnp.broadcast_to(everyone[None], (n_cells, width + B)),
            first_observed,
        ],
        axis=1,
    )
    about_low = about.astype(bf16)
    packet, about_low, about = together((packet, about_low, about))
    packets = exchange(packet, CELL_AXIS)
    group_about = gather(about_low, GENE_AXIS)
    arrived = jnp.sum(packets, axis=0)
    shift = (group_mean - arrived[:width] / n_cells)[None]
    batch_total = arrived[width : width + B][None]
    observed = arrived[width + B :].reshape(piece, B)
    embedding = about + shift
    own_rows = unit(embedding)
    unit_rows = unit(group_about.astype(f32) + shift)
    penalty = penalty_halves(observed, batch_total, total_cells)

    for iteration in range(ITERS):
        if iteration == 0:
            sums = dot(assign, unit_rows)
            sums, own_rows, penalty, embedding = together((sums, own_rows, penalty, embedding))
            sums = jnp.sum(exchange(sums.reshape(n_cells, piece, width), CELL_AXIS), axis=0)
        else:
            weights = weigh(
                dot_rows(rows[:, :width], unit_rows), dot(rows[:, width:], batch_twice)
            )
            norm = jnp.sum(share(jnp.sum(weights, axis=0), GENE_AXIS), axis=0)
            rounded = (weights / norm[None, :]).astype(bf16)
            sums = jnp.concatenate(
                [dot(rounded, unit_rows), dot_rows(rounded, batch_hot)], axis=1
            )
            sums = jnp.sum(exchange(sums.reshape(n_cells, piece, width + B), CELL_AXIS), axis=0)
            penalty = penalty_halves(sums[:, width:], batch_total, total_cells)
            sums = sums[:, :width]
        rows = jnp.concatenate([unit(sums), penalty], axis=1)
        rows = share(rows, CELL_AXIS).reshape(mine, width + 2 * B)

    rows = gather(rows, GENE_AXIS)
    weights = weigh(dot_rows(own_rows, rows[:, :width]), dot_rows(own_twice, rows[:, width:]))
    assign = weights / jnp.sum(weights, axis=1, keepdims=True)
    return (embedding, assign, rows[:, :width])


def solution(mesh):
    placed = (
        P("cells", "genes"),
        P(("cells", "genes"), None),
        P(("cells", "genes"), None),
        P("genes", None),
    )
    return jax.shard_map(
        per_device,
        mesh=mesh,
        in_specs=placed,
        out_specs=(P(("cells", "genes"), None), P(("cells", "genes"), None), P()),
        check_vma=False,
    )
```

```python
import jax
import jax.numpy as jnp
from jax import lax
from jax.sharding import PartitionSpec as P

K = 1024
B = 64
ITERS = 2
CELL_AXIS = "cells"
GENE_AXIS = "genes"

epsilon = 1e-06
cluster_spread = 0.1

f32 = jnp.float32
bf16 = jnp.bfloat16
trailing = (((1,), (1,)), ((), ()))
together = lax.optimization_barrier


def exchange(blocks, axis):
    return lax.all_to_all(blocks, axis, 0, 0, tiled=False)


def share(block, axis):
    return exchange(jnp.broadcast_to(block[None], (lax.axis_size(axis),) + block.shape), axis)


def gather(block, axis):
    return lax.all_gather(block, axis, tiled=True)


def dot(left, right):
    return jnp.dot(left, right, preferred_element_type=f32)


def dot_rows(left, right):
    return lax.dot_general(left, right, trailing, preferred_element_type=f32)


def hot_columns(labels, count):
    return (labels[None, :] == jnp.arange(count, dtype=f32)[:, None]).astype(bf16)


def halves(value):
    high = value.astype(bf16)
    return high, (value - high.astype(f32)).astype(bf16)


def unit(rows):
    scaled = rows * lax.rsqrt(jnp.sum(rows * rows, axis=1, keepdims=True) + epsilon)
    return scaled.astype(bf16)


def penalty_halves(observed, batch_total, total_cells):
    mass = jnp.sum(observed, axis=1, keepdims=True)
    ratio = (mass * batch_total / total_cells + 1.0) / (observed + 1.0)
    return jnp.concatenate(halves(ratio * ratio), axis=1)


def weigh(similarity, lookup):
    distance = 2.0 - 2.0 * similarity
    return jnp.exp(-distance / cluster_spread) * lookup


def per_device(counts, batch, seeds, loadings):
    n_cells, n_genes = lax.axis_size(CELL_AXIS), lax.axis_size(GENE_AXIS)
    group, own = counts.shape[0], batch.shape[0]
    total_cells = group * n_cells
    width = loadings.shape[1]
    mine = K // n_genes
    piece = mine // n_cells

    values = counts.astype(f32)
    shares = dot_rows(jnp.ones((8, counts.shape[1]), bf16), counts.astype(bf16))
    packet = jnp.concatenate([shares[0], batch[:, 0].astype(f32), seeds[:, 0].astype(f32)])
    own_hot = (batch == jnp.arange(B, dtype=jnp.int32)[None, :]).astype(bf16)
    own_twice = jnp.concatenate([own_hot, own_hot], axis=1)
    first = (lax.axis_index(GENE_AXIS) * mine).astype(f32)
    packet, own_twice, first = together((packet, own_twice, first))
    packets = share(packet, GENE_AXIS)
    depth_total = jnp.sum(packets[:, :group], axis=0)
    group_batch = packets[:, group : group + own].reshape(group)
    group_seeds = packets[:, group + own :].reshape(group)

    logged = jnp.log1p(10000.0 * values / depth_total[:, None]).astype(bf16)
    partial = dot(logged, loadings)

    batch_hot = hot_columns(group_batch, B)
    batch_twice = jnp.concatenate([batch_hot, batch_hot], axis=0)
    assign = hot_columns(group_seeds - first, mine)
    first_observed = dot_rows(assign, batch_hot)
    group_labels = dot_rows(jnp.ones((8, group), bf16), batch_hot)[0]

    everyone = jnp.concatenate([jnp.sum(partial, axis=0), group_labels])
    packet = jnp.concatenate(
        [
            jnp.broadcast_to(everyone[None], (n_cells, width + B)),
            first_observed.reshape(n_cells, piece * B),
        ],
        axis=1,
    )
    packet, batch_hot, batch_twice, assign = together((packet, batch_hot, batch_twice, assign))
    arrived = jnp.sum(exchange(packet, CELL_AXIS), axis=0)
    center = arrived[:width] / total_cells
    batch_total = arrived[width : width + B][None]
    observed = arrived[width + B :].reshape(piece, B)
    penalty = penalty_halves(observed, batch_total, total_cells)

    centred = (partial - center[None]).astype(bf16).reshape(n_genes, own, width)
    centred, penalty, batch_total = together((centred, penalty, batch_total))
    embedding = jnp.sum(exchange(centred, GENE_AXIS).astype(f32), axis=0)
    own_rows = unit(embedding)
    unit_rows = gather(own_rows, GENE_AXIS)

    for iteration in range(ITERS):
        if iteration == 0:
            sums = dot(assign, unit_rows)
            sums = jnp.sum(exchange(sums.reshape(n_cells, piece, width), CELL_AXIS), axis=0)
        else:
            weights = weigh(
                dot_rows(rows[:, :width], unit_rows), dot(rows[:, width:], batch_twice)
            )
            norm = jnp.sum(share(jnp.sum(weights, axis=0), GENE_AXIS), axis=0)
            rounded = (weights / norm[None, :]).astype(bf16)
            sums = jnp.concatenate(
                [dot(rounded, unit_rows), dot_rows(rounded, batch_hot)], axis=1
            )
            sums = jnp.sum(exchange(sums.reshape(n_cells, piece, width + B), CELL_AXIS), axis=0)
            penalty = penalty_halves(sums[:, width:], batch_total, total_cells)
            sums = sums[:, :width]
        rows = jnp.concatenate([unit(sums), penalty], axis=1)
        rows = share(rows, CELL_AXIS).reshape(mine, width + 2 * B)

    rows = gather(rows, GENE_AXIS)
    weights = weigh(dot_rows(own_rows, rows[:, :width]), dot_rows(own_twice, rows[:, width:]))
    assign = weights / jnp.sum(weights, axis=1, keepdims=True)
    return (embedding, assign, rows[:, :width])


def solution(mesh):
    placed = (
        P("cells", "genes"),
        P(("cells", "genes"), None),
        P(("cells", "genes"), None),
        P("genes", None),
    )
    return jax.shard_map(
        per_device,
        mesh=mesh,
        in_specs=placed,
        out_specs=(P(("cells", "genes"), None), P(("cells", "genes"), None), P()),
        check_vma=False,
    )
```

```python
import jax
import jax.numpy as jnp
from jax import lax
from jax.sharding import PartitionSpec as P

K = 1024
B = 64
ITERS = 2
CELL_AXIS = "cells"
Z_AXIS = "z"
CORE_AXIS = "core"
GENE_AXIS = (Z_AXIS, CORE_AXIS)

epsilon = 1e-06
cluster_spread = 0.1

f32 = jnp.float32
bf16 = jnp.bfloat16
trailing = (((1,), (1,)), ((), ()))
together = lax.optimization_barrier


def exchange(blocks, axis):
    return lax.all_to_all(blocks, axis, 0, 0, tiled=False)


def share(block, axis):
    return exchange(jnp.broadcast_to(block[None], (lax.axis_size(axis),) + block.shape), axis)


def gather(block, axis):
    return lax.all_gather(block, axis, tiled=True)


def dot(left, right):
    return jnp.dot(left, right, preferred_element_type=f32)


def dot_rows(left, right):
    return lax.dot_general(left, right, trailing, preferred_element_type=f32)


def hot_columns(labels, count):
    return (labels[None, :] == jnp.arange(count, dtype=f32)[:, None]).astype(bf16)


def halves(value):
    high = value.astype(bf16)
    return high, (value - high.astype(f32)).astype(bf16)


def unit(rows):
    scaled = rows * lax.rsqrt(jnp.sum(rows * rows, axis=1, keepdims=True) + epsilon)
    return scaled.astype(bf16)


def penalty_halves(observed, batch_total, total_cells):
    mass = jnp.sum(observed, axis=1, keepdims=True)
    ratio = (mass * batch_total / total_cells + 1.0) / (observed + 1.0)
    return jnp.concatenate(halves(ratio * ratio), axis=1)


def weigh(similarity, lookup):
    distance = 2.0 - 2.0 * similarity
    return jnp.exp(-distance / cluster_spread) * lookup


def per_device(counts, batch, seeds, loadings):
    n_cells, n_genes = lax.axis_size(CELL_AXIS), lax.axis_size(GENE_AXIS)
    n_z, n_core = lax.axis_size(Z_AXIS), lax.axis_size(CORE_AXIS)
    group, own = counts.shape[0], batch.shape[0]
    total_cells = group * n_cells
    width = loadings.shape[1]
    mine = K // n_genes
    piece = mine // n_cells

    values = counts.astype(f32)
    shares = dot_rows(jnp.ones((8, counts.shape[1]), bf16), counts.astype(bf16))
    packet = jnp.concatenate([shares[0], batch[:, 0].astype(f32), seeds[:, 0].astype(f32)])
    own_hot = (batch == jnp.arange(B, dtype=jnp.int32)[None, :]).astype(bf16)
    own_twice = jnp.concatenate([own_hot, own_hot], axis=1)
    first = (lax.axis_index(GENE_AXIS) * mine).astype(f32)
    even = lax.axis_index(CORE_AXIS) == 0
    packet, own_twice, first, even = together((packet, own_twice, first, even))
    packets = share(packet, GENE_AXIS)
    depth_total = jnp.sum(packets[:, :group], axis=0)
    labels = packets[:, group:].reshape(n_z, n_core, 2, own).transpose(2, 1, 0, 3)
    group_batch = labels[0].reshape(group)
    group_seeds = labels[1].reshape(group)

    logged = jnp.log1p(10000.0 * values / depth_total[:, None]).astype(bf16)
    partial = dot(logged, loadings)

    batch_hot = hot_columns(group_batch, B)
    batch_twice = jnp.concatenate([batch_hot, batch_hot], axis=0)
    assign = hot_columns(group_seeds - first, mine)
    first_observed = dot_rows(assign, batch_hot)
    group_labels = dot_rows(jnp.ones((8, group), bf16), batch_hot)[0]

    everyone = jnp.concatenate([jnp.sum(partial, axis=0), group_labels])
    packet = jnp.concatenate(
        [
            jnp.broadcast_to(everyone[None], (n_cells, width + B)),
            first_observed.reshape(n_cells, piece * B),
        ],
        axis=1,
    )
    packet, batch_hot, batch_twice, assign = together((packet, batch_hot, batch_twice, assign))
    arrived = jnp.sum(exchange(packet, CELL_AXIS), axis=0)
    center = arrived[:width] / total_cells
    batch_total = arrived[width : width + B][None]
    observed = arrived[width + B :].reshape(piece, B)
    penalty = penalty_halves(observed, batch_total, total_cells)

    centred = (partial - center[None]).reshape(n_z, n_core, own, width)
    kept = jnp.where(even, centred[:, 0], centred[:, 1])
    given = jnp.where(even, centred[:, 1], centred[:, 0]).astype(bf16)
    given, kept, penalty, batch_total = together((given, kept, penalty, batch_total))
    taken = lax.ppermute(given, CORE_AXIS, [(0, 1), (1, 0)])
    pairs = (kept + taken.astype(f32)).astype(bf16)
    embedding = jnp.sum(exchange(pairs, Z_AXIS).astype(f32), axis=0)
    own_rows = unit(embedding)
    unit_rows = gather(share(own_rows, Z_AXIS).reshape(n_z * own, width), CORE_AXIS)

    for iteration in range(ITERS):
        if iteration == 0:
            sums = dot(assign, unit_rows)
            sums = jnp.sum(exchange(sums.reshape(n_cells, piece, width), CELL_AXIS), axis=0)
        else:
            weights = weigh(
                dot_rows(rows[:, :width], unit_rows), dot(rows[:, width:], batch_twice)
            )
            norm = jnp.sum(share(jnp.sum(weights, axis=0), GENE_AXIS), axis=0)
            rounded = (weights / norm[None, :]).astype(bf16)
            sums = jnp.concatenate(
                [dot(rounded, unit_rows), dot_rows(rounded, batch_hot)], axis=1
            )
            sums = jnp.sum(exchange(sums.reshape(n_cells, piece, width + B), CELL_AXIS), axis=0)
            penalty = penalty_halves(sums[:, width:], batch_total, total_cells)
            sums = sums[:, :width]
        rows = jnp.concatenate([unit(sums), penalty], axis=1)
        rows = share(rows, CELL_AXIS).reshape(mine, width + 2 * B)

    rows = gather(rows, GENE_AXIS)
    weights = weigh(dot_rows(own_rows, rows[:, :width]), dot_rows(own_twice, rows[:, width:]))
    assign = weights / jnp.sum(weights, axis=1, keepdims=True)
    return (embedding, assign, rows[:, :width])


def solution(mesh):
    cells, genes = mesh.devices.shape
    mesh = jax.sharding.Mesh(
        mesh.devices.reshape(cells, genes // 2, 2), (CELL_AXIS, Z_AXIS, CORE_AXIS)
    )
    owners = P((CELL_AXIS, Z_AXIS, CORE_AXIS), None)
    placed = (P(CELL_AXIS, GENE_AXIS), owners, owners, P(GENE_AXIS, None))
    return jax.shard_map(
        per_device,
        mesh=mesh,
        in_specs=placed,
        out_specs=(owners, owners, P()),
        check_vma=False,
    )
```

```python
import jax
import jax.numpy as jnp
from jax import lax
from jax.sharding import PartitionSpec as P

K = 1024
B = 64
ITERS = 2
X_SIZE = 4
Y_AXIS = "y"
X_AXIS = "x"
CELL_AXIS = (Y_AXIS, X_AXIS)
Z_AXIS = "z"
CORE_AXIS = "core"
GENE_AXIS = (Z_AXIS, CORE_AXIS)

epsilon = 1e-06
cluster_spread = 0.1

f32 = jnp.float32
bf16 = jnp.bfloat16
trailing = (((1,), (1,)), ((), ()))
together = lax.optimization_barrier


def exchange(blocks, axis):
    return lax.all_to_all(blocks, axis, 0, 0, tiled=False)


def share(block, axis):
    return exchange(jnp.broadcast_to(block[None], (lax.axis_size(axis),) + block.shape), axis)


def gather(block, axis):
    return lax.all_gather(block, axis, tiled=True)


def dot(left, right):
    return jnp.dot(left, right, preferred_element_type=f32)


def dot_rows(left, right):
    return lax.dot_general(left, right, trailing, preferred_element_type=f32)


def hot_columns(labels, count):
    return (labels[None, :] == jnp.arange(count, dtype=f32)[:, None]).astype(bf16)


def halves(value):
    high = value.astype(bf16)
    return high, (value - high.astype(f32)).astype(bf16)


def unit(rows):
    scaled = rows * lax.rsqrt(jnp.sum(rows * rows, axis=1, keepdims=True) + epsilon)
    return scaled.astype(bf16)


def penalty_halves(observed, batch_total, total_cells):
    mass = jnp.sum(observed, axis=1, keepdims=True)
    ratio = (mass * batch_total / total_cells + 1.0) / (observed + 1.0)
    return jnp.concatenate(halves(ratio * ratio), axis=1)


def added(blocks):
    total = blocks[0].astype(f32)
    for at in range(1, blocks.shape[0]):
        total = total + blocks[at].astype(f32)
    return total


def folded(observed):
    half = observed.shape[0] // 2
    return jnp.concatenate([observed[:half], observed[half:]], axis=1).astype(bf16)


def everywhere(sums, fold):
    half, lanes = sums.shape[0] // 2, sums.shape[1] // 2
    sums = sums.astype(bf16)
    block = jnp.concatenate([sums[:, :lanes], sums[:, lanes:], fold], axis=0)
    for axis in (Y_AXIS, X_AXIS):
        block = added(share(block.astype(bf16), axis))
    sums = jnp.concatenate([block[: 2 * half], block[2 * half : 4 * half]], axis=1)
    observed = jnp.concatenate([block[4 * half :, :B], block[4 * half :, B:]], axis=0)
    return sums, observed


def weigh(similarity, lookup):
    distance = 2.0 - 2.0 * similarity
    return jnp.exp(-distance / cluster_spread) * lookup


def per_device(counts, batch, seeds, loadings):
    n_cells, n_genes = lax.axis_size(CELL_AXIS), lax.axis_size(GENE_AXIS)
    n_z, n_core = lax.axis_size(Z_AXIS), lax.axis_size(CORE_AXIS)
    group, own = counts.shape[0], batch.shape[0]
    total_cells = group * n_cells
    width = loadings.shape[1]
    mine = K // n_genes

    values = counts.astype(f32)
    shares = dot_rows(jnp.ones((8, counts.shape[1]), bf16), counts.astype(bf16))
    packet = jnp.concatenate([shares[0], batch[:, 0].astype(f32), seeds[:, 0].astype(f32)])
    own_hot = (batch == jnp.arange(B, dtype=jnp.int32)[None, :]).astype(bf16)
    own_twice = jnp.concatenate([own_hot, own_hot], axis=1)
    first = (lax.axis_index(GENE_AXIS) * mine).astype(f32)
    even = lax.axis_index(CORE_AXIS) == 0
    packet, own_twice, first, even = together((packet, own_twice, first, even))
    packets = share(packet, GENE_AXIS)
    depth_total = jnp.sum(packets[:, :group], axis=0)
    labels = packets[:, group:].reshape(n_z, n_core, 2, own).transpose(2, 1, 0, 3)
    group_batch = labels[0].reshape(group)
    group_seeds = labels[1].reshape(group)

    logged = jnp.log1p(10000.0 * values / depth_total[:, None]).astype(bf16)
    partial = dot(logged, loadings)

    batch_hot = hot_columns(group_batch, B)
    batch_twice = jnp.concatenate([batch_hot, batch_hot], axis=0)
    assign = hot_columns(group_seeds - first, mine)
    first_fold = folded(dot_rows(assign, batch_hot))
    group_labels = dot_rows(jnp.ones((8, group), bf16), batch_hot)[0]

    packet = jnp.concatenate([jnp.sum(partial, axis=0), group_labels])
    packet, batch_hot, batch_twice, assign, first_fold = together(
        (packet, batch_hot, batch_twice, assign, first_fold)
    )
    arrived = jnp.sum(share(packet, CELL_AXIS), axis=0)
    center = arrived[:width] / total_cells
    batch_total = arrived[width:][None]

    centred = (partial - center[None]).reshape(n_z, n_core, own, width)
    kept = jnp.where(even, centred[:, 0], centred[:, 1])
    given = jnp.where(even, centred[:, 1], centred[:, 0]).astype(bf16)
    given, kept, batch_total = together((given, kept, batch_total))
    taken = lax.ppermute(given, CORE_AXIS, [(0, 1), (1, 0)])
    pairs = (kept + taken.astype(f32)).astype(bf16)
    embedding = jnp.sum(exchange(pairs, Z_AXIS).astype(f32), axis=0)
    own_rows = unit(embedding)
    unit_rows = gather(share(own_rows, Z_AXIS).reshape(n_z * own, width), CORE_AXIS)

    for iteration in range(ITERS):
        if iteration == 0:
            sums, fold = dot(assign, unit_rows), first_fold
        else:
            weights = weigh(dot_rows(rows[:, :width], unit_rows), dot(rows[:, width:], batch_twice))
            norm = jnp.sum(share(jnp.sum(weights, axis=0), GENE_AXIS), axis=0)
            rounded = (weights / norm[None, :]).astype(bf16)
            sums, fold = dot(rounded, unit_rows), folded(dot_rows(rounded, batch_hot))
        sums, observed = everywhere(sums, fold)
        penalty = penalty_halves(observed, batch_total, total_cells)
        rows = jnp.concatenate([unit(sums), penalty], axis=1)

    rows = gather(rows, GENE_AXIS)
    weights = weigh(dot_rows(own_rows, rows[:, :width]), dot_rows(own_twice, rows[:, width:]))
    assign = weights / jnp.sum(weights, axis=1, keepdims=True)
    return (embedding, assign, rows[:, :width])


def solution(mesh):
    cells, genes = mesh.devices.shape
    mesh = jax.sharding.Mesh(
        mesh.devices.reshape(cells // X_SIZE, X_SIZE, genes // 2, 2),
        (Y_AXIS, X_AXIS, Z_AXIS, CORE_AXIS),
    )
    owners = P((Y_AXIS, X_AXIS, Z_AXIS, CORE_AXIS), None)
    placed = (P(CELL_AXIS, GENE_AXIS), owners, owners, P(GENE_AXIS, None))
    return jax.shard_map(
        per_device,
        mesh=mesh,
        in_specs=placed,
        out_specs=(owners, owners, P()),
        check_vma=False,
    )
```

```python
import jax
import jax.numpy as jnp
from jax import lax
from jax.experimental import pallas as pl
from jax.experimental.pallas import tpu as pltpu
from jax.sharding import PartitionSpec as P

K = 1024
B = 64
ITERS = 2
X_SIZE = 4
Y_AXIS = "y"
X_AXIS = "x"
CELL_AXIS = (Y_AXIS, X_AXIS)
Z_AXIS = "z"
CORE_AXIS = "core"
GENE_AXIS = (Z_AXIS, CORE_AXIS)

epsilon = 1e-06
cluster_spread = 0.1

f32 = jnp.float32
bf16 = jnp.bfloat16
trailing = (((1,), (1,)), ((), ()))
together = lax.optimization_barrier


def exchange(blocks, axis):
    return lax.all_to_all(blocks, axis, 0, 0, tiled=False)


def share(block, axis):
    return exchange(jnp.broadcast_to(block[None], (lax.axis_size(axis),) + block.shape), axis)


def gather(block, axis):
    return lax.all_gather(block, axis, tiled=True)


def dot(left, right):
    return jnp.dot(left, right, preferred_element_type=f32)


def dot_rows(left, right):
    return lax.dot_general(left, right, trailing, preferred_element_type=f32)


def hot_columns(labels, count):
    return (labels[None, :] == jnp.arange(count, dtype=f32)[:, None]).astype(bf16)


def halves(value):
    high = value.astype(bf16)
    return high, (value - high.astype(f32)).astype(bf16)


def unit(rows):
    scaled = rows * lax.rsqrt(jnp.sum(rows * rows, axis=1, keepdims=True) + epsilon)
    return scaled.astype(bf16)


def penalty_halves(observed, batch_total, total_cells):
    mass = jnp.sum(observed, axis=1, keepdims=True)
    ratio = (mass * batch_total / total_cells + 1.0) / (observed + 1.0)
    return jnp.concatenate(halves(ratio * ratio), axis=1)


def added(blocks):
    total = blocks[0].astype(f32)
    for at in range(1, blocks.shape[0]):
        total = total + blocks[at].astype(f32)
    return total


def folded(observed):
    half = observed.shape[0] // 2
    return jnp.concatenate([observed[:half], observed[half:]], axis=1).astype(bf16)


def everywhere(sums, fold):
    half, lanes = sums.shape[0] // 2, sums.shape[1] // 2
    sums = sums.astype(bf16)
    block = jnp.concatenate([sums[:, :lanes], sums[:, lanes:], fold], axis=0)
    for axis in (Y_AXIS, X_AXIS):
        block = added(share(block.astype(bf16), axis))
    sums = jnp.concatenate([block[: 2 * half], block[2 * half : 4 * half]], axis=1)
    observed = jnp.concatenate([block[4 * half :, :B], block[4 * half :, B:]], axis=0)
    return sums, observed


def weigh(similarity, lookup):
    distance = 2.0 - 2.0 * similarity
    return jnp.exp(-distance / cluster_spread) * lookup


def start_kernel(counts_hbm, shares_ref, low_ref, held, sems):
    rows = held.shape[1]
    copies = [
        pltpu.make_async_copy(counts_hbm.at[pl.ds(at * rows, rows)], held.at[at], sems.at[at])
        for at in range(held.shape[0])
    ]
    for copy in copies:
        copy.start()
    ones = jnp.ones((8, held.shape[2]), bf16)
    for at, copy in enumerate(copies):
        copy.wait()
        low = held[at].astype(f32).astype(bf16)
        low_ref[pl.ds(at * rows, rows), :] = low
        shares_ref[:, pl.ds(at * rows, rows)] = dot_rows(ones, low)


def start(counts):
    group, genes = counts.shape
    chunks = 4
    return pl.pallas_call(
        start_kernel,
        out_shape=(
            jax.ShapeDtypeStruct((8, group), f32),
            jax.ShapeDtypeStruct((group, genes), bf16),
        ),
        in_specs=[pl.BlockSpec(memory_space=pltpu.HBM)],
        out_specs=(pl.BlockSpec(memory_space=pltpu.VMEM),) * 2,
        scratch_shapes=[
            pltpu.VMEM((chunks, group // chunks, genes), jnp.int32),
            pltpu.SemaphoreType.DMA((chunks,)),
        ],
        compiler_params=pltpu.CompilerParams(vmem_limit_bytes=8 << 20),
    )(pltpu.with_memory_space_constraint(counts, pltpu.HBM))


def finish_kernel(
    own_ref, twice_ref, rows_ref, emb_ref, emb_hbm, assign_hbm, cent_hbm, held, sems
):
    width = own_ref.shape[1]
    copies = [
        pltpu.make_async_copy(rows_ref.at[:, pl.ds(0, width)], cent_hbm, sems.at[0]),
        pltpu.make_async_copy(emb_ref, emb_hbm, sems.at[1]),
    ]
    for copy in copies:
        copy.start()
    similarity = dot_rows(own_ref[...], rows_ref[:, :width])
    lookup = dot_rows(twice_ref[...], rows_ref[:, width:])
    weights = weigh(similarity, lookup)
    total = jnp.sum(weights, axis=1, keepdims=True)
    rows = held.shape[0] // 4
    for at in range(4):
        part = pl.ds(at * rows, rows)
        held[part, :] = weights[at * rows : (at + 1) * rows] / total[at * rows : (at + 1) * rows]
        copy = pltpu.make_async_copy(held.at[part], assign_hbm.at[part], sems.at[2 + at])
        copy.start()
        copies.append(copy)
    for copy in copies:
        copy.wait()


def finish(own_rows, own_twice, rows, embedding):
    own, width = own_rows.shape
    outside = pl.BlockSpec(memory_space=pltpu.HBM)
    return pl.pallas_call(
        finish_kernel,
        out_shape=(
            jax.ShapeDtypeStruct((own, width), f32),
            jax.ShapeDtypeStruct((own, K), f32),
            jax.ShapeDtypeStruct((K, width), bf16),
        ),
        in_specs=[pl.BlockSpec(memory_space=pltpu.VMEM)] * 4,
        out_specs=(outside,) * 3,
        scratch_shapes=[pltpu.VMEM((own, K), f32), pltpu.SemaphoreType.DMA((6,))],
        compiler_params=pltpu.CompilerParams(vmem_limit_bytes=8 << 20),
    )(own_rows, own_twice, rows, embedding)


def per_device(counts, batch, seeds, loadings):
    n_cells, n_genes = lax.axis_size(CELL_AXIS), lax.axis_size(GENE_AXIS)
    n_z, n_core = lax.axis_size(Z_AXIS), lax.axis_size(CORE_AXIS)
    group, own = counts.shape[0], batch.shape[0]
    total_cells = group * n_cells
    width = loadings.shape[1]
    mine = K // n_genes

    shares, values = start(counts)
    packet = jnp.concatenate([shares[0], batch[:, 0].astype(f32), seeds[:, 0].astype(f32)])
    own_hot = (batch == jnp.arange(B, dtype=jnp.int32)[None, :]).astype(bf16)
    own_twice = jnp.concatenate([own_hot, own_hot], axis=1)
    first = (lax.axis_index(GENE_AXIS) * mine).astype(f32)
    even = lax.axis_index(CORE_AXIS) == 0
    packet, own_twice, first, even = together((packet, own_twice, first, even))
    packets = share(packet, GENE_AXIS)
    depth_total = jnp.sum(packets[:, :group], axis=0)
    labels = packets[:, group:].reshape(n_z, n_core, 2, own).transpose(2, 1, 0, 3)
    group_batch = labels[0].reshape(group)
    group_seeds = labels[1].reshape(group)

    logged = jnp.log1p(10000.0 * values.astype(f32) / depth_total[:, None]).astype(bf16)
    partial = dot(logged, loadings)

    batch_hot = hot_columns(group_batch, B)
    batch_twice = jnp.concatenate([batch_hot, batch_hot], axis=0)
    assign = hot_columns(group_seeds - first, mine)
    first_fold = folded(dot_rows(assign, batch_hot))
    group_labels = dot_rows(jnp.ones((8, group), bf16), batch_hot)[0]

    packet = jnp.concatenate([jnp.sum(partial, axis=0), group_labels])
    packet, batch_hot, batch_twice, assign, first_fold = together(
        (packet, batch_hot, batch_twice, assign, first_fold)
    )
    arrived = jnp.sum(share(packet, CELL_AXIS), axis=0)
    center = arrived[:width] / total_cells
    batch_total = arrived[width:][None]

    centred = (partial - center[None]).reshape(n_z, n_core, own, width)
    kept = jnp.where(even, centred[:, 0], centred[:, 1])
    given = jnp.where(even, centred[:, 1], centred[:, 0]).astype(bf16)
    given, kept, batch_total = together((given, kept, batch_total))
    taken = lax.ppermute(given, CORE_AXIS, [(0, 1), (1, 0)])
    pairs = (kept + taken.astype(f32)).astype(bf16)
    embedding = jnp.sum(exchange(pairs, Z_AXIS).astype(f32), axis=0)
    own_rows = unit(embedding)
    unit_rows = gather(share(own_rows, Z_AXIS).reshape(n_z * own, width), CORE_AXIS)

    for iteration in range(ITERS):
        if iteration == 0:
            sums, fold = dot(assign, unit_rows), first_fold
        else:
            weights = weigh(dot_rows(rows[:, :width], unit_rows), dot(rows[:, width:], batch_twice))
            norm = jnp.sum(share(jnp.sum(weights, axis=0), GENE_AXIS), axis=0)
            rounded = (weights / norm[None, :]).astype(bf16)
            sums, fold = dot(rounded, unit_rows), folded(dot_rows(rounded, batch_hot))
        sums, observed = everywhere(sums, fold)
        penalty = penalty_halves(observed, batch_total, total_cells)
        rows = jnp.concatenate([unit(sums), penalty], axis=1)

    rows = gather(rows, GENE_AXIS)
    return finish(own_rows, own_twice, rows, embedding)


def solution(mesh):
    cells, genes = mesh.devices.shape
    mesh = jax.sharding.Mesh(
        mesh.devices.reshape(cells // X_SIZE, X_SIZE, genes // 2, 2),
        (Y_AXIS, X_AXIS, Z_AXIS, CORE_AXIS),
    )
    owners = P((Y_AXIS, X_AXIS, Z_AXIS, CORE_AXIS), None)
    placed = (P(CELL_AXIS, GENE_AXIS), owners, owners, P(GENE_AXIS, None))
    return jax.shard_map(
        per_device,
        mesh=mesh,
        in_specs=placed,
        out_specs=(owners, owners, P()),
        check_vma=False,
    )
```

```python
import jax
import jax.numpy as jnp
from jax import lax
from jax.experimental import pallas as pl
from jax.experimental.pallas import tpu as pltpu
from jax.sharding import PartitionSpec as P

K = 1024
B = 64
ITERS = 2
X_SIZE = 4
Y_AXIS = "y"
X_AXIS = "x"
CELL_AXIS = (Y_AXIS, X_AXIS)
Z_AXIS = "z"
CORE_AXIS = "core"
GENE_AXIS = (Z_AXIS, CORE_AXIS)

epsilon = 1e-06
cluster_spread = 0.1

f32 = jnp.float32
bf16 = jnp.bfloat16
trailing = (((1,), (1,)), ((), ()))
together = lax.optimization_barrier


def exchange(blocks, axis):
    return lax.all_to_all(blocks, axis, 0, 0, tiled=False)


def share(block, axis):
    return exchange(jnp.broadcast_to(block[None], (lax.axis_size(axis),) + block.shape), axis)


def gather(block, axis):
    return lax.all_gather(block, axis, tiled=True)


def dot(left, right):
    return jnp.dot(left, right, preferred_element_type=f32)


def dot_rows(left, right):
    return lax.dot_general(left, right, trailing, preferred_element_type=f32)


def hot_columns(labels, count):
    return (labels[None, :] == jnp.arange(count, dtype=f32)[:, None]).astype(bf16)


def halves(value):
    high = value.astype(bf16)
    return high, (value - high.astype(f32)).astype(bf16)


def unit(rows):
    scaled = rows * lax.rsqrt(jnp.sum(rows * rows, axis=1, keepdims=True) + epsilon)
    return scaled.astype(bf16)


def penalty_halves(observed, batch_total, total_cells):
    mass = jnp.sum(observed, axis=1, keepdims=True)
    ratio = (mass * batch_total / total_cells + 1.0) / (observed + 1.0)
    return jnp.concatenate(halves(ratio * ratio), axis=1)


def added(blocks):
    total = blocks[0].astype(f32)
    for at in range(1, blocks.shape[0]):
        total = total + blocks[at].astype(f32)
    return total


def folded(observed):
    half = observed.shape[0] // 2
    return jnp.concatenate([observed[:half], observed[half:]], axis=1).astype(bf16)


def everywhere(sums, fold):
    half, lanes = sums.shape[0] // 2, sums.shape[1] // 2
    sums = sums.astype(bf16)
    block = jnp.concatenate([sums[:, :lanes], sums[:, lanes:], fold], axis=0)
    for axis in (Y_AXIS, X_AXIS):
        block = added(share(block.astype(bf16), axis))
    sums = jnp.concatenate([block[: 2 * half], block[2 * half : 4 * half]], axis=1)
    observed = jnp.concatenate([block[4 * half :, :B], block[4 * half :, B:]], axis=0)
    return sums, observed


def weigh(similarity, lookup):
    distance = 2.0 - 2.0 * similarity
    return jnp.exp(-distance / cluster_spread) * lookup


def finish_kernel(
    own_ref, twice_ref, rows_ref, emb_ref, emb_hbm, assign_hbm, cent_hbm, held, sems
):
    width = own_ref.shape[1]
    copies = [
        pltpu.make_async_copy(rows_ref.at[:, pl.ds(0, width)], cent_hbm, sems.at[0]),
        pltpu.make_async_copy(emb_ref, emb_hbm, sems.at[1]),
    ]
    for copy in copies:
        copy.start()
    similarity = dot_rows(own_ref[...], rows_ref[:, :width])
    lookup = dot_rows(twice_ref[...], rows_ref[:, width:])
    weights = weigh(similarity, lookup)
    total = jnp.sum(weights, axis=1, keepdims=True)
    rows = held.shape[0] // 4
    for at in range(4):
        part = pl.ds(at * rows, rows)
        held[part, :] = weights[at * rows : (at + 1) * rows] / total[at * rows : (at + 1) * rows]
        copy = pltpu.make_async_copy(held.at[part], assign_hbm.at[part], sems.at[2 + at])
        copy.start()
        copies.append(copy)
    for copy in copies:
        copy.wait()


def finish(own_rows, own_twice, rows, embedding):
    own, width = own_rows.shape
    outside = pl.BlockSpec(memory_space=pltpu.HBM)
    return pl.pallas_call(
        finish_kernel,
        out_shape=(
            jax.ShapeDtypeStruct((own, width), f32),
            jax.ShapeDtypeStruct((own, K), f32),
            jax.ShapeDtypeStruct((K, width), bf16),
        ),
        in_specs=[pl.BlockSpec(memory_space=pltpu.VMEM)] * 4,
        out_specs=(outside,) * 3,
        scratch_shapes=[pltpu.VMEM((own, K), f32), pltpu.SemaphoreType.DMA((6,))],
        compiler_params=pltpu.CompilerParams(vmem_limit_bytes=8 << 20),
    )(own_rows, own_twice, rows, embedding)


def per_device(counts, batch, seeds, loadings):
    n_cells, n_genes = lax.axis_size(CELL_AXIS), lax.axis_size(GENE_AXIS)
    n_z, n_core = lax.axis_size(Z_AXIS), lax.axis_size(CORE_AXIS)
    group, own = counts.shape[0], batch.shape[0]
    total_cells = group * n_cells
    width = loadings.shape[1]
    mine = K // n_genes

    values = counts.astype(f32)
    shares = dot_rows(jnp.ones((8, counts.shape[1]), bf16), counts.astype(bf16))
    packet = jnp.concatenate([shares[0], batch[:, 0].astype(f32), seeds[:, 0].astype(f32)])
    own_hot = (batch == jnp.arange(B, dtype=jnp.int32)[None, :]).astype(bf16)
    own_twice = jnp.concatenate([own_hot, own_hot], axis=1)
    first = (lax.axis_index(GENE_AXIS) * mine).astype(f32)
    even = lax.axis_index(CORE_AXIS) == 0
    packet, own_twice, first, even = together((packet, own_twice, first, even))
    packets = share(packet, GENE_AXIS)
    depth_total = jnp.sum(packets[:, :group], axis=0)
    labels = packets[:, group:].reshape(n_z, n_core, 2, own).transpose(2, 1, 0, 3)
    group_batch = labels[0].reshape(group)
    group_seeds = labels[1].reshape(group)

    logged = jnp.log1p(10000.0 * values / depth_total[:, None]).astype(bf16)
    partial = dot(logged, loadings)

    batch_hot = hot_columns(group_batch, B)
    batch_twice = jnp.concatenate([batch_hot, batch_hot], axis=0)
    assign = hot_columns(group_seeds - first, mine)
    first_fold = folded(dot_rows(assign, batch_hot))
    group_labels = dot_rows(jnp.ones((8, group), bf16), batch_hot)[0]

    packet = jnp.concatenate([jnp.sum(partial, axis=0), group_labels])
    packet, batch_hot, batch_twice, assign, first_fold = together(
        (packet, batch_hot, batch_twice, assign, first_fold)
    )
    arrived = jnp.sum(share(packet, CELL_AXIS), axis=0)
    center = arrived[:width] / total_cells
    batch_total = arrived[width:][None]

    centred = (partial - center[None]).reshape(n_z, n_core, own, width)
    kept = jnp.where(even, centred[:, 0], centred[:, 1])
    given = jnp.where(even, centred[:, 1], centred[:, 0]).astype(bf16)
    given, kept, batch_total = together((given, kept, batch_total))
    both = lax.all_gather(given, CORE_AXIS)
    taken = jnp.where(even, both[1], both[0])
    pairs = (kept + taken.astype(f32)).astype(bf16)
    embedding = jnp.sum(exchange(pairs, Z_AXIS).astype(f32), axis=0)
    own_rows = unit(embedding)
    unit_rows = gather(share(own_rows, Z_AXIS).reshape(n_z * own, width), CORE_AXIS)

    for iteration in range(ITERS):
        if iteration == 0:
            sums, fold = dot(assign, unit_rows), first_fold
        else:
            weights = weigh(dot_rows(rows[:, :width], unit_rows), dot(rows[:, width:], batch_twice))
            norm = jnp.sum(share(jnp.sum(weights, axis=0), GENE_AXIS), axis=0)
            rounded = (weights / norm[None, :]).astype(bf16)
            sums, fold = dot(rounded, unit_rows), folded(dot_rows(rounded, batch_hot))
        sums, observed = everywhere(sums, fold)
        penalty = penalty_halves(observed, batch_total, total_cells)
        rows = jnp.concatenate([unit(sums), penalty], axis=1)

    rows = gather(rows, GENE_AXIS)
    return finish(own_rows, own_twice, rows, embedding)


def solution(mesh):
    cells, genes = mesh.devices.shape
    mesh = jax.sharding.Mesh(
        mesh.devices.reshape(cells // X_SIZE, X_SIZE, genes // 2, 2),
        (Y_AXIS, X_AXIS, Z_AXIS, CORE_AXIS),
    )
    owners = P((Y_AXIS, X_AXIS, Z_AXIS, CORE_AXIS), None)
    placed = (P(CELL_AXIS, GENE_AXIS), owners, owners, P(GENE_AXIS, None))
    return jax.shard_map(
        per_device,
        mesh=mesh,
        in_specs=placed,
        out_specs=(owners, owners, P()),
        check_vma=False,
    )
```

```python
from functools import partial as partial_of

import jax
import jax.numpy as jnp
from jax import lax
from jax.experimental import pallas as pl
from jax.experimental.pallas import tpu as pltpu
from jax.sharding import PartitionSpec as P

K = 1024
B = 64
ITERS = 2
X_SIZE = 4
Y_AXIS = "y"
X_AXIS = "x"
CELL_AXIS = (Y_AXIS, X_AXIS)
Z_AXIS = "z"
CORE_AXIS = "core"
GENE_AXIS = (Z_AXIS, CORE_AXIS)

epsilon = 1e-06
cluster_spread = 0.1

f32 = jnp.float32
bf16 = jnp.bfloat16
trailing = (((1,), (1,)), ((), ()))
together = lax.optimization_barrier


def exchange(blocks, axis):
    return lax.all_to_all(blocks, axis, 0, 0, tiled=False)


def share(block, axis):
    return exchange(jnp.broadcast_to(block[None], (lax.axis_size(axis),) + block.shape), axis)


def gather(block, axis):
    return lax.all_gather(block, axis, tiled=True)


def dot(left, right):
    return jnp.dot(left, right, preferred_element_type=f32)


def dot_rows(left, right):
    return lax.dot_general(left, right, trailing, preferred_element_type=f32)


def hot_columns(labels, count):
    return (labels[None, :] == jnp.arange(count, dtype=f32)[:, None]).astype(bf16)


def halves(value):
    high = value.astype(bf16)
    return high, (value - high.astype(f32)).astype(bf16)


def unit(rows):
    scaled = rows * lax.rsqrt(jnp.sum(rows * rows, axis=1, keepdims=True) + epsilon)
    return scaled.astype(bf16)


def added(blocks):
    total = blocks[0].astype(f32)
    for at in range(1, blocks.shape[0]):
        total = total + blocks[at].astype(f32)
    return total


def folded(observed):
    half = observed.shape[0] // 2
    return jnp.concatenate([observed[:half], observed[half:]], axis=1).astype(bf16)


def block_of(sums, fold):
    lanes = sums.shape[1] // 2
    sums = sums.astype(bf16)
    return jnp.concatenate([sums[:, :lanes], sums[:, lanes:], fold], axis=0)


def everywhere(block):
    return share(added(share(block, Y_AXIS)).astype(bf16), X_AXIS)


def weigh(similarity, lookup):
    distance = 2.0 - 2.0 * similarity
    return jnp.exp(-distance / cluster_spread) * lookup


def tables(blocks_ref, twice_ref, total_cells, clusters):
    total = added(blocks_ref)
    left, right = total[:clusters], total[clusters : 2 * clusters]
    observed = total[2 * clusters :]
    scale = lax.rsqrt(jnp.sum(left * left + right * right, axis=1, keepdims=True) + epsilon)
    unit_rows = jnp.concatenate([left * scale, right * scale], axis=1).astype(bf16)
    low_lanes = lax.broadcasted_iota(jnp.int32, observed.shape, 1) < B
    zero = jnp.zeros_like(observed)
    mass = jnp.where(
        low_lanes,
        jnp.sum(jnp.where(low_lanes, observed, zero), axis=1, keepdims=True),
        jnp.sum(jnp.where(low_lanes, zero, observed), axis=1, keepdims=True),
    )
    ratio = (mass * twice_ref[...] / total_cells + 1.0) / (observed + 1.0)
    high, low = halves(ratio * ratio)
    return unit_rows, high.astype(f32), low.astype(f32), low_lanes


def weights_kernel(total_cells, blocks_ref, twice_ref, rows_ref, hot_ref, weights_ref, sum_ref):
    clusters = weights_ref.shape[0]
    centroids, high, low, low_lanes = tables(blocks_ref, twice_ref, total_cells, clusters)
    zero = jnp.zeros_like(high)
    upper = jnp.concatenate(
        [jnp.where(low_lanes, high, zero), jnp.where(low_lanes, low, zero)], axis=1
    )
    lower = jnp.concatenate(
        [jnp.where(low_lanes, zero, high), jnp.where(low_lanes, zero, low)], axis=1
    )
    penalty = jnp.concatenate([upper, lower], axis=0).astype(bf16)
    weights = weigh(dot_rows(centroids, rows_ref[...]), dot(penalty, hot_ref[...]))
    weights_ref[...] = weights
    sum_ref[...] = jnp.sum(weights, axis=0, keepdims=True)


def sums_kernel(weights_ref, norm_ref, rows_ref, hot_ref, block_ref):
    clusters, lanes = weights_ref.shape[0], rows_ref.shape[1] // 2
    rounded = (weights_ref[...] / norm_ref[...]).astype(bf16)
    sums = dot(rounded, rows_ref[...])
    observed = dot_rows(rounded, hot_ref[: 2 * B, :])
    half = clusters // 2
    low_lanes = lax.broadcasted_iota(jnp.int32, (half, 2 * B), 1) < B
    block_ref[:clusters, :] = sums[:, :lanes].astype(bf16)
    block_ref[clusters : 2 * clusters, :] = sums[:, lanes:].astype(bf16)
    block_ref[2 * clusters :, :] = jnp.where(
        low_lanes, observed[:half], observed[half:]
    ).astype(bf16)


def pack_kernel(total_cells, blocks_ref, twice_ref, rows_ref):
    clusters, width = rows_ref.shape[0], rows_ref.shape[1] - 2 * B
    centroids, high, low, low_lanes = tables(blocks_ref, twice_ref, total_cells, clusters)
    rows_ref[:, :width] = centroids
    upper = jnp.where(low_lanes, high, pltpu.roll(low, B, 1))
    lower = jnp.where(low_lanes, pltpu.roll(high, B, 1), low)
    rows_ref[:, width:] = jnp.concatenate([upper, lower], axis=0).astype(bf16)


def local(kernel, shapes, *operands):
    inside = pl.BlockSpec(memory_space=pltpu.VMEM)
    return pl.pallas_call(
        kernel,
        out_shape=shapes,
        in_specs=[inside] * len(operands),
        out_specs=jax.tree.map(lambda _: inside, shapes),
        compiler_params=pltpu.CompilerParams(vmem_limit_bytes=8 << 20),
    )(*operands)


def finish_kernel(
    own_ref, twice_ref, rows_ref, emb_ref, emb_hbm, assign_hbm, cent_hbm, held, sems
):
    width = own_ref.shape[1]
    copies = [
        pltpu.make_async_copy(rows_ref.at[:, pl.ds(0, width)], cent_hbm, sems.at[0]),
        pltpu.make_async_copy(emb_ref, emb_hbm, sems.at[1]),
    ]
    for copy in copies:
        copy.start()
    similarity = dot_rows(own_ref[...], rows_ref[:, :width])
    lookup = dot_rows(twice_ref[...], rows_ref[:, width:])
    weights = weigh(similarity, lookup)
    total = jnp.sum(weights, axis=1, keepdims=True)
    rows = held.shape[0] // 4
    for at in range(4):
        part = pl.ds(at * rows, rows)
        held[part, :] = weights[at * rows : (at + 1) * rows] / total[at * rows : (at + 1) * rows]
        copy = pltpu.make_async_copy(held.at[part], assign_hbm.at[part], sems.at[2 + at])
        copy.start()
        copies.append(copy)
    for copy in copies:
        copy.wait()


def finish(own_rows, own_twice, rows, embedding):
    own, width = own_rows.shape
    outside = pl.BlockSpec(memory_space=pltpu.HBM)
    return pl.pallas_call(
        finish_kernel,
        out_shape=(
            jax.ShapeDtypeStruct((own, width), f32),
            jax.ShapeDtypeStruct((own, K), f32),
            jax.ShapeDtypeStruct((K, width), bf16),
        ),
        in_specs=[pl.BlockSpec(memory_space=pltpu.VMEM)] * 4,
        out_specs=(outside,) * 3,
        scratch_shapes=[pltpu.VMEM((own, K), f32), pltpu.SemaphoreType.DMA((6,))],
        compiler_params=pltpu.CompilerParams(vmem_limit_bytes=8 << 20),
    )(own_rows, own_twice, rows, embedding)


def per_device(counts, batch, seeds, loadings):
    n_cells, n_genes = lax.axis_size(CELL_AXIS), lax.axis_size(GENE_AXIS)
    n_z, n_core = lax.axis_size(Z_AXIS), lax.axis_size(CORE_AXIS)
    group, own = counts.shape[0], batch.shape[0]
    total_cells = group * n_cells
    width = loadings.shape[1]
    mine = K // n_genes

    values = counts.astype(f32)
    shares = dot_rows(jnp.ones((8, counts.shape[1]), bf16), counts.astype(bf16))
    packet = jnp.concatenate([shares[0], batch[:, 0].astype(f32), seeds[:, 0].astype(f32)])
    first = (lax.axis_index(GENE_AXIS) * mine).astype(f32)
    even = lax.axis_index(CORE_AXIS) == 0
    own_hot = (batch == jnp.arange(B, dtype=jnp.int32)[None, :]).astype(bf16)
    own_twice = jnp.concatenate([own_hot, own_hot], axis=1)
    packet, own_twice, first, even = together((packet, own_twice, first, even))
    packets = share(packet, GENE_AXIS)
    depth_total = jnp.sum(packets[:, :group], axis=0)
    labels = packets[:, group:].reshape(n_z, n_core, 2, own).transpose(2, 1, 0, 3)
    group_batch = labels[0].reshape(group)
    group_seeds = labels[1].reshape(group)

    logged = jnp.log1p(10000.0 * values / depth_total[:, None]).astype(bf16)
    partial = dot(logged, loadings)

    batch_hot = hot_columns(group_batch, B)
    hot_four = jnp.concatenate([batch_hot] * 4, axis=0)
    assign = hot_columns(group_seeds - first, mine)
    first_fold = folded(dot_rows(assign, batch_hot))
    group_labels = dot_rows(jnp.ones((8, group), bf16), batch_hot)[0]
    packet = jnp.concatenate([jnp.sum(partial, axis=0), group_labels])
    packet, hot_four, assign, first_fold = together((packet, hot_four, assign, first_fold))
    arrived = jnp.sum(share(packet, CELL_AXIS), axis=0)
    center = arrived[:width] / total_cells
    twice_total = jnp.concatenate([arrived[width:], arrived[width:]])[None]

    centred = (partial - center[None]).reshape(n_z, n_core, own, width)
    kept = jnp.where(even, centred[:, 0], centred[:, 1])
    given = jnp.where(even, centred[:, 1], centred[:, 0]).astype(bf16)
    given, kept, twice_total = together((given, kept, twice_total))
    both = lax.all_gather(given, CORE_AXIS)
    taken = jnp.where(even, both[1], both[0])
    pairs = (kept + taken.astype(f32)).astype(bf16)
    embedding = jnp.sum(exchange(pairs, Z_AXIS).astype(f32), axis=0)
    own_rows = unit(embedding)
    unit_rows = gather(share(own_rows, Z_AXIS).reshape(n_z * own, width), CORE_AXIS)

    blocks = everywhere(block_of(dot(assign, unit_rows), first_fold))
    for _ in range(1, ITERS):
        weights, shares = local(
            partial_of(weights_kernel, total_cells),
            (jax.ShapeDtypeStruct((mine, group), f32), jax.ShapeDtypeStruct((1, group), f32)),
            blocks,
            twice_total,
            unit_rows,
            hot_four,
        )
        norm = jnp.sum(share(shares, GENE_AXIS), axis=0)
        block = local(
            sums_kernel,
            jax.ShapeDtypeStruct(blocks.shape[1:], bf16),
            weights,
            norm,
            unit_rows,
            hot_four,
        )
        blocks = everywhere(block)

    rows = local(
        partial_of(pack_kernel, total_cells),
        jax.ShapeDtypeStruct((mine, width + 2 * B), bf16),
        blocks,
        twice_total,
    )
    rows = gather(rows, GENE_AXIS)
    return finish(own_rows, own_twice, rows, embedding)


def solution(mesh):
    cells, genes = mesh.devices.shape
    mesh = jax.sharding.Mesh(
        mesh.devices.reshape(cells // X_SIZE, X_SIZE, genes // 2, 2),
        (Y_AXIS, X_AXIS, Z_AXIS, CORE_AXIS),
    )
    owners = P((Y_AXIS, X_AXIS, Z_AXIS, CORE_AXIS), None)
    placed = (P(CELL_AXIS, GENE_AXIS), owners, owners, P(GENE_AXIS, None))
    return jax.shard_map(
        per_device,
        mesh=mesh,
        in_specs=placed,
        out_specs=(owners, owners, P()),
        check_vma=False,
    )
```

```python
from functools import partial as partial_of

import jax
import jax.numpy as jnp
from jax import lax
from jax.experimental import pallas as pl
from jax.experimental.pallas import tpu as pltpu
from jax.sharding import PartitionSpec as P

K = 1024
B = 64
ITERS = 2
X_SIZE = 4
Y_AXIS = "y"
X_AXIS = "x"
CELL_AXIS = (Y_AXIS, X_AXIS)
Z_AXIS = "z"
CORE_AXIS = "core"
GENE_AXIS = (Z_AXIS, CORE_AXIS)

epsilon = 1e-06
cluster_spread = 0.1

f32 = jnp.float32
bf16 = jnp.bfloat16
trailing = (((1,), (1,)), ((), ()))
together = lax.optimization_barrier


def exchange(blocks, axis):
    return lax.all_to_all(blocks, axis, 0, 0, tiled=False)


def share(block, axis):
    return exchange(jnp.broadcast_to(block[None], (lax.axis_size(axis),) + block.shape), axis)


def gather(block, axis):
    return lax.all_gather(block, axis, tiled=True)


def dot(left, right):
    return jnp.dot(left, right, preferred_element_type=f32)


def dot_rows(left, right):
    return lax.dot_general(left, right, trailing, preferred_element_type=f32)


def halves(value):
    high = value.astype(bf16)
    return high, (value - high.astype(f32)).astype(bf16)


def unit(rows):
    scaled = rows * lax.rsqrt(jnp.sum(rows * rows, axis=1, keepdims=True) + epsilon)
    return scaled.astype(bf16)


def added(blocks):
    total = blocks[0].astype(f32)
    for at in range(1, blocks.shape[0]):
        total = total + blocks[at].astype(f32)
    return total


def block_of(sums, beside):
    lanes = sums.shape[1] // 2
    sums = sums.astype(bf16)
    return jnp.concatenate([sums[:, :lanes], sums[:, lanes:], beside], axis=0)


def everywhere(block):
    return share(added(share(block, Y_AXIS)).astype(bf16), X_AXIS)


def weigh(similarity, lookup):
    distance = 2.0 - 2.0 * similarity
    return jnp.exp(-distance / cluster_spread) * lookup


def tables(sums, observed, twice_ref, total_cells):
    clusters = sums.shape[0] // 2
    left, right = sums[:clusters], sums[clusters:]
    scale = lax.rsqrt(jnp.sum(left * left + right * right, axis=1, keepdims=True) + epsilon)
    unit_rows = jnp.concatenate([left * scale, right * scale], axis=1).astype(bf16)
    low_lanes = lax.broadcasted_iota(jnp.int32, observed.shape, 1) < B
    zero = jnp.zeros_like(observed)
    mass = jnp.where(
        low_lanes,
        jnp.sum(jnp.where(low_lanes, observed, zero), axis=1, keepdims=True),
        jnp.sum(jnp.where(low_lanes, zero, observed), axis=1, keepdims=True),
    )
    ratio = (mass * twice_ref[...] / total_cells + 1.0) / (observed + 1.0)
    high, low = halves(ratio * ratio)
    return unit_rows, high.astype(f32), low.astype(f32), low_lanes


def labels_kernel(labels_ref, hot_ref, assign_ref, fold_ref, twice_ref):
    group = labels_ref.shape[1]
    batch, seeds = labels_ref[0:1, :], labels_ref[1:2, :]

    def hot(labels, row):
        return (labels.astype(jnp.int32) == row).astype(f32).astype(bf16)

    def iota(count):
        return lax.broadcasted_iota(jnp.int32, (count, group), 0)

    twice = hot(batch, iota(2 * B) % B)
    hot_ref[: 2 * B, :] = twice
    hot_ref[2 * B :, :] = twice
    clusters = assign_ref.shape[0]
    assign_ref[...] = hot(seeds, iota(clusters))
    half = clusters // 2
    row = iota(half)
    row = (row % X_SIZE) * (half // X_SIZE) + row // X_SIZE
    low_lanes = lax.broadcasted_iota(jnp.int32, (half, 2 * B), 1) < B
    fold_ref[...] = jnp.where(
        low_lanes,
        dot_rows(hot(seeds, row), twice),
        dot_rows(hot(seeds, row + half), twice),
    )
    twice_ref[...] = dot_rows(jnp.ones((8, group), bf16), twice)


def weights_kernel(total_cells, blocks_ref, twice_ref, rows_ref, hot_ref, weights_ref, sum_ref):
    sums = 2 * weights_ref.shape[0]
    rows = (blocks_ref.shape[1] - sums) // 2
    observed = jnp.concatenate(
        [
            blocks_ref[at, sums : sums + rows].astype(f32)
            + blocks_ref[at, sums + rows :].astype(f32)
            for at in range(blocks_ref.shape[0])
        ],
        axis=0,
    )
    total = added(blocks_ref)[:sums]
    centroids, high, low, low_lanes = tables(total, observed, twice_ref, total_cells)
    zero = jnp.zeros_like(high)
    upper = jnp.concatenate(
        [jnp.where(low_lanes, high, zero), jnp.where(low_lanes, low, zero)], axis=1
    )
    lower = jnp.concatenate(
        [jnp.where(low_lanes, zero, high), jnp.where(low_lanes, zero, low)], axis=1
    )
    penalty = jnp.concatenate([upper, lower], axis=0).astype(bf16)
    weights = weigh(dot_rows(centroids, rows_ref[...]), dot(penalty, hot_ref[...]))
    weights_ref[...] = weights
    sum_ref[...] = jnp.sum(weights, axis=0, keepdims=True)


def sums_kernel(weights_ref, norm_ref, rows_ref, hot_ref, block_ref):
    clusters, lanes = weights_ref.shape[0], rows_ref.shape[1] // 2
    rounded = (weights_ref[...] / norm_ref[...]).astype(bf16)
    sums = dot(rounded, rows_ref[...])
    observed = dot_rows(rounded, hot_ref[: 2 * B, :])
    half = clusters // 2
    low_lanes = lax.broadcasted_iota(jnp.int32, (half, 2 * B), 1) < B
    block_ref[:clusters, :] = sums[:, :lanes].astype(bf16)
    block_ref[clusters : 2 * clusters, :] = sums[:, lanes:].astype(bf16)
    block_ref[2 * clusters :, :] = jnp.where(
        low_lanes, observed[:half], observed[half:]
    ).astype(bf16)


def pack_kernel(total_cells, blocks_ref, twice_ref, rows_ref):
    clusters, width = rows_ref.shape[0], rows_ref.shape[1] - 2 * B
    total = added(blocks_ref)
    centroids, high, low, low_lanes = tables(
        total[: 2 * clusters], total[2 * clusters :], twice_ref, total_cells
    )
    rows_ref[:, :width] = centroids
    upper = jnp.where(low_lanes, high, pltpu.roll(low, B, 1))
    lower = jnp.where(low_lanes, pltpu.roll(high, B, 1), low)
    rows_ref[:, width:] = jnp.concatenate([upper, lower], axis=0).astype(bf16)


def local(kernel, shapes, *operands):
    inside = pl.BlockSpec(memory_space=pltpu.VMEM)
    return pl.pallas_call(
        kernel,
        out_shape=shapes,
        in_specs=[inside] * len(operands),
        out_specs=jax.tree.map(lambda _: inside, shapes),
        compiler_params=pltpu.CompilerParams(vmem_limit_bytes=8 << 20),
    )(*operands)


def finish_kernel(
    own_ref, twice_ref, rows_ref, emb_ref, emb_hbm, assign_hbm, cent_hbm, held, sems
):
    width = own_ref.shape[1]
    copies = [
        pltpu.make_async_copy(rows_ref.at[:, pl.ds(0, width)], cent_hbm, sems.at[0]),
        pltpu.make_async_copy(emb_ref, emb_hbm, sems.at[1]),
    ]
    for copy in copies:
        copy.start()
    similarity = dot_rows(own_ref[...], rows_ref[:, :width])
    lookup = dot_rows(twice_ref[...], rows_ref[:, width:])
    weights = weigh(similarity, lookup)
    total = jnp.sum(weights, axis=1, keepdims=True)
    rows = held.shape[0] // 4
    for at in range(4):
        part = pl.ds(at * rows, rows)
        held[part, :] = weights[at * rows : (at + 1) * rows] / total[at * rows : (at + 1) * rows]
        copy = pltpu.make_async_copy(held.at[part], assign_hbm.at[part], sems.at[2 + at])
        copy.start()
        copies.append(copy)
    for copy in copies:
        copy.wait()


def finish(own_rows, own_twice, rows, embedding):
    own, width = own_rows.shape
    outside = pl.BlockSpec(memory_space=pltpu.HBM)
    return pl.pallas_call(
        finish_kernel,
        out_shape=(
            jax.ShapeDtypeStruct((own, width), f32),
            jax.ShapeDtypeStruct((own, K), f32),
            jax.ShapeDtypeStruct((K, width), bf16),
        ),
        in_specs=[pl.BlockSpec(memory_space=pltpu.VMEM)] * 4,
        out_specs=(outside,) * 3,
        scratch_shapes=[pltpu.VMEM((own, K), f32), pltpu.SemaphoreType.DMA((6,))],
        compiler_params=pltpu.CompilerParams(vmem_limit_bytes=8 << 20),
    )(own_rows, own_twice, rows, embedding)


def per_device(counts, batch, seeds, loadings):
    n_cells, n_genes = lax.axis_size(CELL_AXIS), lax.axis_size(GENE_AXIS)
    n_z, n_core = lax.axis_size(Z_AXIS), lax.axis_size(CORE_AXIS)
    group, own = counts.shape[0], batch.shape[0]
    total_cells = group * n_cells
    width = loadings.shape[1]
    mine = K // n_genes

    values = counts.astype(f32)
    shares = dot_rows(jnp.ones((8, counts.shape[1]), bf16), counts.astype(bf16))
    packet = jnp.concatenate([shares[0], batch[:, 0].astype(f32), seeds[:, 0].astype(f32)])
    first = (lax.axis_index(GENE_AXIS) * mine).astype(f32)
    even = lax.axis_index(CORE_AXIS) == 0
    own_hot = (batch == jnp.arange(B, dtype=jnp.int32)[None, :]).astype(bf16)
    own_twice = jnp.concatenate([own_hot, own_hot], axis=1)
    packet, own_twice, first, even = together((packet, own_twice, first, even))
    packets = share(packet, GENE_AXIS)
    depth_total = jnp.sum(packets[:, :group], axis=0)
    labels = packets[:, group:].reshape(n_z, n_core, 2, own).transpose(2, 1, 0, 3)
    labels = jnp.stack([labels[0].reshape(group), labels[1].reshape(group) - first])
    hot_four, assign, fold, group_labels = local(
        labels_kernel,
        (
            jax.ShapeDtypeStruct((4 * B, group), bf16),
            jax.ShapeDtypeStruct((mine, group), bf16),
            jax.ShapeDtypeStruct((mine // 2, 2 * B), f32),
            jax.ShapeDtypeStruct((8, 2 * B), f32),
        ),
        labels,
    )

    logged = jnp.log1p(10000.0 * values / depth_total[:, None]).astype(bf16)
    partial = dot(logged, loadings)

    everyone = jnp.concatenate([jnp.sum(partial, axis=0), group_labels[0]])
    packet = jnp.concatenate(
        [jnp.broadcast_to(everyone[None], (n_cells, width + 2 * B)), fold], axis=1
    )
    packet, hot_four, assign = together((packet, hot_four, assign))
    arrived = jnp.sum(exchange(packet, CELL_AXIS), axis=0)
    center = arrived[:width] / total_cells
    twice_total = arrived[width : width + 2 * B][None]
    high, low = halves(arrived[width + 2 * B :][None])
    counted = jnp.concatenate([high] * 4 + [low] * 4, axis=0)

    centred = (partial - center[None]).reshape(n_z, n_core, own, width)
    kept = jnp.where(even, centred[:, 0], centred[:, 1])
    given = jnp.where(even, centred[:, 1], centred[:, 0]).astype(bf16)
    given, kept, twice_total, counted = together((given, kept, twice_total, counted))
    both = lax.all_gather(given, CORE_AXIS)
    taken = jnp.where(even, both[1], both[0])
    pairs = (kept + taken.astype(f32)).astype(bf16)
    embedding = jnp.sum(exchange(pairs, Z_AXIS).astype(f32), axis=0)
    own_rows = unit(embedding)
    unit_rows = gather(share(own_rows, Z_AXIS).reshape(n_z * own, width), CORE_AXIS)

    arrived = share(block_of(dot(assign, unit_rows), counted), Y_AXIS)
    sums = added(arrived[:, : 2 * mine]).astype(bf16)
    blocks = jnp.concatenate([sums, arrived[:, 2 * mine], arrived[:, 2 * mine + 4]], axis=0)
    blocks = share(blocks, X_AXIS)
    for _ in range(1, ITERS):
        weights, shares = local(
            partial_of(weights_kernel, total_cells),
            (jax.ShapeDtypeStruct((mine, group), f32), jax.ShapeDtypeStruct((1, group), f32)),
            blocks,
            twice_total,
            unit_rows,
            hot_four,
        )
        norm = jnp.sum(share(shares, GENE_AXIS), axis=0)
        block = local(
            sums_kernel,
            jax.ShapeDtypeStruct((2 * mine + mine // 2, 2 * B), bf16),
            weights,
            norm,
            unit_rows,
            hot_four,
        )
        blocks = everywhere(block)

    rows = local(
        partial_of(pack_kernel, total_cells),
        jax.ShapeDtypeStruct((mine, width + 2 * B), bf16),
        blocks,
        twice_total,
    )
    rows = gather(rows, GENE_AXIS)
    return finish(own_rows, own_twice, rows, embedding)


def solution(mesh):
    cells, genes = mesh.devices.shape
    mesh = jax.sharding.Mesh(
        mesh.devices.reshape(cells // X_SIZE, X_SIZE, genes // 2, 2),
        (Y_AXIS, X_AXIS, Z_AXIS, CORE_AXIS),
    )
    owners = P((Y_AXIS, X_AXIS, Z_AXIS, CORE_AXIS), None)
    placed = (P(CELL_AXIS, GENE_AXIS), owners, owners, P(GENE_AXIS, None))
    return jax.shard_map(
        per_device,
        mesh=mesh,
        in_specs=placed,
        out_specs=(owners, owners, P()),
        check_vma=False,
    )
```

```python
from functools import partial as partial_of

import jax
import jax.numpy as jnp
from jax import lax
from jax.experimental import pallas as pl
from jax.experimental.pallas import tpu as pltpu
from jax.sharding import PartitionSpec as P

K = 1024
B = 64
ITERS = 2
X_SIZE = 4
Y_AXIS = "y"
X_AXIS = "x"
CELL_AXIS = (Y_AXIS, X_AXIS)
Z_AXIS = "z"
CORE_AXIS = "core"
GENE_AXIS = (Z_AXIS, CORE_AXIS)

epsilon = 1e-06
cluster_spread = 0.1

f32 = jnp.float32
bf16 = jnp.bfloat16
trailing = (((1,), (1,)), ((), ()))
together = lax.optimization_barrier


def exchange(blocks, axis):
    return lax.all_to_all(blocks, axis, 0, 0, tiled=False)


def share(block, axis):
    return exchange(jnp.broadcast_to(block[None], (lax.axis_size(axis),) + block.shape), axis)


def gather(block, axis):
    return lax.all_gather(block, axis, tiled=True)


def dot(left, right):
    return jnp.dot(left, right, preferred_element_type=f32)


def dot_rows(left, right):
    return lax.dot_general(left, right, trailing, preferred_element_type=f32)


def halves(value):
    high = value.astype(bf16)
    return high, (value - high.astype(f32)).astype(bf16)


def unit(rows):
    scaled = rows * lax.rsqrt(jnp.sum(rows * rows, axis=1, keepdims=True) + epsilon)
    return scaled.astype(bf16)


def added(blocks):
    total = blocks[0].astype(f32)
    for at in range(1, blocks.shape[0]):
        total = total + blocks[at].astype(f32)
    return total


def block_of(sums, beside):
    lanes = sums.shape[1] // 2
    sums = sums.astype(bf16)
    return jnp.concatenate([sums[:, :lanes], sums[:, lanes:], beside], axis=0)


def everywhere(block):
    return share(added(share(block, Y_AXIS)).astype(bf16), X_AXIS)


def weigh(similarity, lookup):
    distance = 2.0 - 2.0 * similarity
    return jnp.exp(-distance / cluster_spread) * lookup


def tables(sums, observed, twice_ref, total_cells):
    clusters = sums.shape[0] // 2
    left, right = sums[:clusters], sums[clusters:]
    scale = lax.rsqrt(jnp.sum(left * left + right * right, axis=1, keepdims=True) + epsilon)
    unit_rows = jnp.concatenate([left * scale, right * scale], axis=1).astype(bf16)
    low_lanes = lax.broadcasted_iota(jnp.int32, observed.shape, 1) < B
    zero = jnp.zeros_like(observed)
    mass = jnp.where(
        low_lanes,
        jnp.sum(jnp.where(low_lanes, observed, zero), axis=1, keepdims=True),
        jnp.sum(jnp.where(low_lanes, zero, observed), axis=1, keepdims=True),
    )
    ratio = (mass * twice_ref[...] / total_cells + 1.0) / (observed + 1.0)
    high, low = halves(ratio * ratio)
    return unit_rows, high.astype(f32), low.astype(f32), low_lanes


def labels_kernel(labels_ref, hot_ref, assign_ref, fold_ref, twice_ref):
    group = labels_ref.shape[1]
    batch, seeds = labels_ref[0:1, :], labels_ref[1:2, :]

    def hot(labels, row):
        return (labels.astype(jnp.int32) == row).astype(f32).astype(bf16)

    def iota(count):
        return lax.broadcasted_iota(jnp.int32, (count, group), 0)

    twice = hot(batch, iota(2 * B) % B)
    hot_ref[: 2 * B, :] = twice
    hot_ref[2 * B :, :] = twice
    clusters = assign_ref.shape[0]
    assign_ref[...] = hot(seeds, iota(clusters))
    half = clusters // 2
    row = iota(half)
    row = (row % X_SIZE) * (half // X_SIZE) + row // X_SIZE
    low_lanes = lax.broadcasted_iota(jnp.int32, (half, 2 * B), 1) < B
    fold_ref[...] = jnp.where(
        low_lanes,
        dot_rows(hot(seeds, row), twice),
        dot_rows(hot(seeds, row + half), twice),
    )
    twice_ref[...] = dot_rows(jnp.ones((8, group), bf16), twice)


def weights_kernel(total_cells, blocks_ref, twice_ref, rows_ref, hot_ref, weights_ref, sum_ref):
    sums = 2 * weights_ref.shape[0]
    rows = (blocks_ref.shape[1] - sums) // 2
    observed = jnp.concatenate(
        [
            blocks_ref[at, sums : sums + rows].astype(f32)
            + blocks_ref[at, sums + rows :].astype(f32)
            for at in range(blocks_ref.shape[0])
        ],
        axis=0,
    )
    total = added(blocks_ref)[:sums]
    centroids, high, low, low_lanes = tables(total, observed, twice_ref, total_cells)
    zero = jnp.zeros_like(high)
    upper = jnp.concatenate(
        [jnp.where(low_lanes, high, zero), jnp.where(low_lanes, low, zero)], axis=1
    )
    lower = jnp.concatenate(
        [jnp.where(low_lanes, zero, high), jnp.where(low_lanes, zero, low)], axis=1
    )
    penalty = jnp.concatenate([upper, lower], axis=0).astype(bf16)
    weights = weigh(dot_rows(centroids, rows_ref[...]), dot(penalty, hot_ref[...]))
    weights_ref[...] = weights
    sum_ref[...] = jnp.sum(weights, axis=0, keepdims=True)


def sums_kernel(weights_ref, norm_ref, rows_ref, hot_ref, block_ref):
    clusters, lanes = weights_ref.shape[0], rows_ref.shape[1] // 2
    rounded = (weights_ref[...] / norm_ref[...]).astype(bf16)
    sums = dot(rounded, rows_ref[...])
    observed = dot_rows(rounded, hot_ref[: 2 * B, :])
    half = clusters // 2
    low_lanes = lax.broadcasted_iota(jnp.int32, (half, 2 * B), 1) < B
    block_ref[:clusters, :] = sums[:, :lanes].astype(bf16)
    block_ref[clusters : 2 * clusters, :] = sums[:, lanes:].astype(bf16)
    block_ref[2 * clusters :, :] = jnp.where(
        low_lanes, observed[:half], observed[half:]
    ).astype(bf16)


def pack_kernel(total_cells, blocks_ref, twice_ref, packed_ref):
    sums = packed_ref.shape[0] * 4 // 5
    half = sums // 2
    total = added(blocks_ref)
    centroids, high, _, _ = tables(total[:sums], total[sums:], twice_ref, total_cells)
    lanes = centroids.shape[1] // 2
    packed_ref[:half, :] = centroids[:, :lanes]
    packed_ref[half:sums, :] = centroids[:, lanes:]
    packed_ref[sums:, :] = high.astype(bf16)


def local(kernel, shapes, *operands):
    inside = pl.BlockSpec(memory_space=pltpu.VMEM)
    return pl.pallas_call(
        kernel,
        out_shape=shapes,
        in_specs=[inside] * len(operands),
        out_specs=jax.tree.map(lambda _: inside, shapes),
        compiler_params=pltpu.CompilerParams(vmem_limit_bytes=8 << 20),
    )(*operands)


def finish_kernel(
    own_ref, twice_ref, packed_ref, emb_ref, emb_hbm, assign_hbm, cent_hbm, cent, held, sems
):
    lanes = packed_ref.shape[2]
    clusters = cent.shape[0] // packed_ref.shape[0]
    left = packed_ref[:, :clusters, :].reshape(K, lanes)
    right = packed_ref[:, clusters : 2 * clusters, :].reshape(K, lanes)
    cent[:, :lanes] = left
    cent[:, lanes:] = right
    copies = [
        pltpu.make_async_copy(cent, cent_hbm, sems.at[0]),
        pltpu.make_async_copy(emb_ref, emb_hbm, sems.at[1]),
    ]
    for copy in copies:
        copy.start()
    similarity = dot_rows(own_ref[:, :lanes], left) + dot_rows(own_ref[:, lanes:], right)
    fold = packed_ref[:, 2 * clusters :, :].astype(f32)
    low_lanes = lax.broadcasted_iota(jnp.int32, fold.shape, 2) < B
    zero = jnp.zeros_like(fold)
    penalty = jnp.concatenate(
        [jnp.where(low_lanes, fold, zero), jnp.where(low_lanes, zero, fold)], axis=1
    )
    lookup = dot_rows(twice_ref[...], penalty.reshape(K, lanes).astype(bf16))
    weights = weigh(similarity, lookup)
    total = jnp.sum(weights, axis=1, keepdims=True)
    rows = held.shape[0] // 4
    for at in range(4):
        part = pl.ds(at * rows, rows)
        held[part, :] = weights[at * rows : (at + 1) * rows] / total[at * rows : (at + 1) * rows]
        copy = pltpu.make_async_copy(held.at[part], assign_hbm.at[part], sems.at[2 + at])
        copy.start()
        copies.append(copy)
    for copy in copies:
        copy.wait()


def finish(own_rows, own_twice, packed, embedding):
    own, width = own_rows.shape
    outside = pl.BlockSpec(memory_space=pltpu.HBM)
    return pl.pallas_call(
        finish_kernel,
        out_shape=(
            jax.ShapeDtypeStruct((own, width), f32),
            jax.ShapeDtypeStruct((own, K), f32),
            jax.ShapeDtypeStruct((K, width), bf16),
        ),
        in_specs=[pl.BlockSpec(memory_space=pltpu.VMEM)] * 4,
        out_specs=(outside,) * 3,
        scratch_shapes=[
            pltpu.VMEM((K, width), bf16),
            pltpu.VMEM((own, K), f32),
            pltpu.SemaphoreType.DMA((6,)),
        ],
        compiler_params=pltpu.CompilerParams(vmem_limit_bytes=8 << 20),
    )(own_rows, own_twice, packed, embedding)


def per_device(counts, batch, seeds, loadings):
    n_cells, n_genes = lax.axis_size(CELL_AXIS), lax.axis_size(GENE_AXIS)
    n_z, n_core = lax.axis_size(Z_AXIS), lax.axis_size(CORE_AXIS)
    group, own = counts.shape[0], batch.shape[0]
    total_cells = group * n_cells
    width = loadings.shape[1]
    mine = K // n_genes

    values = counts.astype(f32)
    shares = dot_rows(jnp.ones((8, counts.shape[1]), bf16), counts.astype(bf16))
    packet = jnp.concatenate([shares[0], batch[:, 0].astype(f32), seeds[:, 0].astype(f32)])
    first = (lax.axis_index(GENE_AXIS) * mine).astype(f32)
    even = lax.axis_index(CORE_AXIS) == 0
    own_hot = (batch == jnp.arange(B, dtype=jnp.int32)[None, :]).astype(bf16)
    own_twice = jnp.concatenate([own_hot, own_hot], axis=1)
    packet, own_twice, first, even = together((packet, own_twice, first, even))
    packets = share(packet, GENE_AXIS)
    depth_total = jnp.sum(packets[:, :group], axis=0)
    labels = packets[:, group:].reshape(n_z, n_core, 2, own).transpose(2, 1, 0, 3)
    labels = jnp.stack([labels[0].reshape(group), labels[1].reshape(group) - first])
    hot_four, assign, fold, group_labels = local(
        labels_kernel,
        (
            jax.ShapeDtypeStruct((4 * B, group), bf16),
            jax.ShapeDtypeStruct((mine, group), bf16),
            jax.ShapeDtypeStruct((mine // 2, 2 * B), f32),
            jax.ShapeDtypeStruct((8, 2 * B), f32),
        ),
        labels,
    )

    logged = jnp.log1p(10000.0 * values / depth_total[:, None]).astype(bf16)
    partial = dot(logged, loadings)

    everyone = jnp.concatenate([jnp.sum(partial, axis=0), group_labels[0]])
    packet = jnp.concatenate(
        [jnp.broadcast_to(everyone[None], (n_cells, width + 2 * B)), fold], axis=1
    )
    packet, hot_four, assign = together((packet, hot_four, assign))
    arrived = jnp.sum(exchange(packet, CELL_AXIS), axis=0)
    center = arrived[:width] / total_cells
    twice_total = arrived[width : width + 2 * B][None]
    high, low = halves(arrived[width + 2 * B :][None])
    counted = jnp.concatenate([high] * 4 + [low] * 4, axis=0)

    centred = (partial - center[None]).reshape(n_z, n_core, own, width)
    kept = jnp.where(even, centred[:, 0], centred[:, 1])
    given = jnp.where(even, centred[:, 1], centred[:, 0]).astype(bf16)
    given, kept, twice_total, counted = together((given, kept, twice_total, counted))
    both = lax.all_gather(given, CORE_AXIS)
    taken = jnp.where(even, both[1], both[0])
    pairs = (kept + taken.astype(f32)).astype(bf16)
    embedding = jnp.sum(exchange(pairs, Z_AXIS).astype(f32), axis=0)
    own_rows = unit(embedding)
    unit_rows = gather(share(own_rows, Z_AXIS).reshape(n_z * own, width), CORE_AXIS)

    arrived = share(block_of(dot(assign, unit_rows), counted), Y_AXIS)
    sums = added(arrived[:, : 2 * mine]).astype(bf16)
    blocks = jnp.concatenate([sums, arrived[:, 2 * mine], arrived[:, 2 * mine + 4]], axis=0)
    blocks = share(blocks, X_AXIS)
    for _ in range(1, ITERS):
        weights, shares = local(
            partial_of(weights_kernel, total_cells),
            (jax.ShapeDtypeStruct((mine, group), f32), jax.ShapeDtypeStruct((1, group), f32)),
            blocks,
            twice_total,
            unit_rows,
            hot_four,
        )
        norm = jnp.sum(share(shares, GENE_AXIS), axis=0)
        block = local(
            sums_kernel,
            jax.ShapeDtypeStruct((2 * mine + mine // 2, 2 * B), bf16),
            weights,
            norm,
            unit_rows,
            hot_four,
        )
        blocks = everywhere(block)

    packed = local(
        partial_of(pack_kernel, total_cells),
        jax.ShapeDtypeStruct(blocks.shape[1:], bf16),
        blocks,
        twice_total,
    )
    packed = gather(packed, GENE_AXIS).reshape((n_genes,) + packed.shape)
    return finish(own_rows, own_twice, packed, embedding)


def solution(mesh):
    cells, genes = mesh.devices.shape
    mesh = jax.sharding.Mesh(
        mesh.devices.reshape(cells // X_SIZE, X_SIZE, genes // 2, 2),
        (Y_AXIS, X_AXIS, Z_AXIS, CORE_AXIS),
    )
    owners = P((Y_AXIS, X_AXIS, Z_AXIS, CORE_AXIS), None)
    placed = (P(CELL_AXIS, GENE_AXIS), owners, owners, P(GENE_AXIS, None))
    return jax.shard_map(
        per_device,
        mesh=mesh,
        in_specs=placed,
        out_specs=(owners, owners, P()),
        check_vma=False,
    )
```

```python
from functools import partial as partial_of

import jax
import jax.numpy as jnp
from jax import lax
from jax.experimental import pallas as pl
from jax.experimental.pallas import tpu as pltpu
from jax.sharding import PartitionSpec as P

K = 1024
B = 64
ITERS = 2
X_SIZE = 4
Y_AXIS = "y"
X_AXIS = "x"
CELL_AXIS = (Y_AXIS, X_AXIS)
Z_AXIS = "z"
CORE_AXIS = "core"
GENE_AXIS = (Z_AXIS, CORE_AXIS)

epsilon = 1e-06
cluster_spread = 0.1

f32 = jnp.float32
bf16 = jnp.bfloat16
trailing = (((1,), (1,)), ((), ()))
together = lax.optimization_barrier


def exchange(blocks, axis):
    return lax.all_to_all(blocks, axis, 0, 0, tiled=False)


def share(block, axis):
    return exchange(jnp.broadcast_to(block[None], (lax.axis_size(axis),) + block.shape), axis)


def gather(block, axis):
    return lax.all_gather(block, axis, tiled=True)


def dot(left, right):
    return jnp.dot(left, right, preferred_element_type=f32)


def dot_rows(left, right):
    return lax.dot_general(left, right, trailing, preferred_element_type=f32)


def halves(value):
    high = value.astype(bf16)
    return high, (value - high.astype(f32)).astype(bf16)


def unit(rows):
    scaled = rows * lax.rsqrt(jnp.sum(rows * rows, axis=1, keepdims=True) + epsilon)
    return scaled.astype(bf16)


def added(blocks):
    total = blocks[0].astype(f32)
    for at in range(1, blocks.shape[0]):
        total = total + blocks[at].astype(f32)
    return total


def block_of(sums, beside):
    lanes = sums.shape[1] // 2
    sums = sums.astype(bf16)
    return jnp.concatenate([sums[:, :lanes], sums[:, lanes:], beside], axis=0)


def everywhere(block):
    return share(added(share(block, Y_AXIS)).astype(bf16), X_AXIS)


def weigh(similarity, lookup):
    distance = 2.0 - 2.0 * similarity
    return jnp.exp(-distance / cluster_spread) * lookup


def tables(sums, observed, twice_ref, total_cells):
    clusters = sums.shape[0] // 2
    left, right = sums[:clusters], sums[clusters:]
    scale = lax.rsqrt(jnp.sum(left * left + right * right, axis=1, keepdims=True) + epsilon)
    unit_rows = jnp.concatenate([left * scale, right * scale], axis=1).astype(bf16)
    low_lanes = lax.broadcasted_iota(jnp.int32, observed.shape, 1) < B
    zero = jnp.zeros_like(observed)
    mass = jnp.where(
        low_lanes,
        jnp.sum(jnp.where(low_lanes, observed, zero), axis=1, keepdims=True),
        jnp.sum(jnp.where(low_lanes, zero, observed), axis=1, keepdims=True),
    )
    ratio = (mass * twice_ref[...] / total_cells + 1.0) / (observed + 1.0)
    high, low = halves(ratio * ratio)
    return unit_rows, high.astype(f32), low.astype(f32), low_lanes


def labels_kernel(labels_ref, hot_ref, assign_ref, fold_ref, twice_ref):
    group = assign_ref.shape[1]
    given = labels_ref[...]
    turned = pltpu.roll(given, B, 1)
    low = lax.broadcasted_iota(jnp.int32, (1, 2 * B), 1) < B
    batch, seeds = [], []
    for core in range(2):
        for at in range(core, given.shape[0], 4):
            here, there = slice(at, at + 1), slice(at + 2, at + 3)
            batch.append(jnp.where(low, given[here], turned[there]))
            seeds.append(jnp.where(low, turned[here], given[there]))
    batch = jnp.concatenate(batch, axis=1)
    own = lax.axis_index(Z_AXIS) * lax.axis_size(CORE_AXIS) + lax.axis_index(CORE_AXIS)
    seeds = jnp.concatenate(seeds, axis=1) - (own * assign_ref.shape[0]).astype(f32)

    def hot(labels, row):
        return (labels.astype(jnp.int32) == row).astype(f32).astype(bf16)

    def iota(count):
        return lax.broadcasted_iota(jnp.int32, (count, group), 0)

    twice = hot(batch, iota(2 * B) % B)
    hot_ref[: 2 * B, :] = twice
    hot_ref[2 * B :, :] = twice
    clusters = assign_ref.shape[0]
    assign_ref[...] = hot(seeds, iota(clusters))
    half = clusters // 2
    row = iota(half)
    row = (row % X_SIZE) * (half // X_SIZE) + row // X_SIZE
    low_lanes = lax.broadcasted_iota(jnp.int32, (half, 2 * B), 1) < B
    fold_ref[...] = jnp.where(
        low_lanes,
        dot_rows(hot(seeds, row), twice),
        dot_rows(hot(seeds, row + half), twice),
    )
    twice_ref[...] = dot_rows(jnp.ones((8, group), bf16), twice)


def weights_kernel(total_cells, blocks_ref, twice_ref, rows_ref, hot_ref, weights_ref, sum_ref):
    sums = 2 * weights_ref.shape[0]
    rows = (blocks_ref.shape[1] - sums) // 2
    observed = jnp.concatenate(
        [
            blocks_ref[at, sums : sums + rows].astype(f32)
            + blocks_ref[at, sums + rows :].astype(f32)
            for at in range(blocks_ref.shape[0])
        ],
        axis=0,
    )
    total = added(blocks_ref)[:sums]
    centroids, high, low, low_lanes = tables(total, observed, twice_ref, total_cells)
    zero = jnp.zeros_like(high)
    upper = jnp.concatenate(
        [jnp.where(low_lanes, high, zero), jnp.where(low_lanes, low, zero)], axis=1
    )
    lower = jnp.concatenate(
        [jnp.where(low_lanes, zero, high), jnp.where(low_lanes, zero, low)], axis=1
    )
    penalty = jnp.concatenate([upper, lower], axis=0).astype(bf16)
    weights = weigh(dot_rows(centroids, rows_ref[...]), dot(penalty, hot_ref[...]))
    weights_ref[...] = weights
    sum_ref[...] = jnp.sum(weights, axis=0, keepdims=True)


def sums_kernel(weights_ref, norm_ref, rows_ref, hot_ref, block_ref):
    clusters, lanes = weights_ref.shape[0], rows_ref.shape[1] // 2
    rounded = (weights_ref[...] / norm_ref[...]).astype(bf16)
    sums = dot(rounded, rows_ref[...])
    observed = dot_rows(rounded, hot_ref[: 2 * B, :])
    half = clusters // 2
    low_lanes = lax.broadcasted_iota(jnp.int32, (half, 2 * B), 1) < B
    block_ref[:clusters, :] = sums[:, :lanes].astype(bf16)
    block_ref[clusters : 2 * clusters, :] = sums[:, lanes:].astype(bf16)
    block_ref[2 * clusters :, :] = jnp.where(
        low_lanes, observed[:half], observed[half:]
    ).astype(bf16)


def pack_kernel(total_cells, blocks_ref, twice_ref, rows_ref):
    clusters, width = rows_ref.shape[0], rows_ref.shape[1] - 2 * B
    total = added(blocks_ref)
    centroids, high, low, low_lanes = tables(
        total[: 2 * clusters], total[2 * clusters :], twice_ref, total_cells
    )
    rows_ref[:, :width] = centroids
    upper = jnp.where(low_lanes, high, pltpu.roll(low, B, 1))
    lower = jnp.where(low_lanes, pltpu.roll(high, B, 1), low)
    rows_ref[:, width:] = jnp.concatenate([upper, lower], axis=0).astype(bf16)


def local(kernel, shapes, *operands):
    inside = pl.BlockSpec(memory_space=pltpu.VMEM)
    return pl.pallas_call(
        kernel,
        out_shape=shapes,
        in_specs=[inside] * len(operands),
        out_specs=jax.tree.map(lambda _: inside, shapes),
        compiler_params=pltpu.CompilerParams(vmem_limit_bytes=8 << 20),
    )(*operands)


def finish_kernel(
    own_ref, twice_ref, rows_ref, emb_ref, emb_hbm, assign_hbm, cent_hbm, held, sems
):
    width = own_ref.shape[1]
    copies = [
        pltpu.make_async_copy(rows_ref.at[:, pl.ds(0, width)], cent_hbm, sems.at[0]),
        pltpu.make_async_copy(emb_ref, emb_hbm, sems.at[1]),
    ]
    for copy in copies:
        copy.start()
    similarity = dot_rows(own_ref[...], rows_ref[:, :width])
    lookup = dot_rows(twice_ref[...], rows_ref[:, width:])
    weights = weigh(similarity, lookup)
    total = jnp.sum(weights, axis=1, keepdims=True)
    rows = held.shape[0] // 4
    for at in range(4):
        part = pl.ds(at * rows, rows)
        held[part, :] = weights[at * rows : (at + 1) * rows] / total[at * rows : (at + 1) * rows]
        copy = pltpu.make_async_copy(held.at[part], assign_hbm.at[part], sems.at[2 + at])
        copy.start()
        copies.append(copy)
    for copy in copies:
        copy.wait()


def finish(own_rows, own_twice, rows, embedding):
    own, width = own_rows.shape
    outside = pl.BlockSpec(memory_space=pltpu.HBM)
    return pl.pallas_call(
        finish_kernel,
        out_shape=(
            jax.ShapeDtypeStruct((own, width), f32),
            jax.ShapeDtypeStruct((own, K), f32),
            jax.ShapeDtypeStruct((K, width), bf16),
        ),
        in_specs=[pl.BlockSpec(memory_space=pltpu.VMEM)] * 4,
        out_specs=(outside,) * 3,
        scratch_shapes=[pltpu.VMEM((own, K), f32), pltpu.SemaphoreType.DMA((6,))],
        compiler_params=pltpu.CompilerParams(vmem_limit_bytes=8 << 20),
    )(own_rows, own_twice, rows, embedding)


def per_device(counts, batch, seeds, loadings):
    n_cells, n_genes = lax.axis_size(CELL_AXIS), lax.axis_size(GENE_AXIS)
    n_z, n_core = lax.axis_size(Z_AXIS), lax.axis_size(CORE_AXIS)
    group, own = counts.shape[0], batch.shape[0]
    total_cells = group * n_cells
    width = loadings.shape[1]
    mine = K // n_genes

    values = counts.astype(f32)
    shares = dot_rows(jnp.ones((8, counts.shape[1]), bf16), counts.astype(bf16))
    packet = jnp.concatenate([shares[0], batch[:, 0].astype(f32), seeds[:, 0].astype(f32)])
    even = lax.axis_index(CORE_AXIS) == 0
    own_hot = (batch == jnp.arange(B, dtype=jnp.int32)[None, :]).astype(bf16)
    own_twice = jnp.concatenate([own_hot, own_hot], axis=1)
    packet, own_twice, even = together((packet, own_twice, even))
    packets = share(packet, GENE_AXIS)
    depth_total = jnp.sum(packets[:, :group], axis=0)
    hot_four, assign, fold, group_labels = local(
        labels_kernel,
        (
            jax.ShapeDtypeStruct((4 * B, group), bf16),
            jax.ShapeDtypeStruct((mine, group), bf16),
            jax.ShapeDtypeStruct((mine // 2, 2 * B), f32),
            jax.ShapeDtypeStruct((8, 2 * B), f32),
        ),
        packets[:, group:],
    )

    logged = jnp.log1p(10000.0 * values / depth_total[:, None]).astype(bf16)
    partial = dot(logged, loadings)

    everyone = jnp.concatenate([jnp.sum(partial, axis=0), group_labels[0]])
    packet = jnp.concatenate(
        [jnp.broadcast_to(everyone[None], (n_cells, width + 2 * B)), fold], axis=1
    )
    packet, hot_four, assign = together((packet, hot_four, assign))
    arrived = jnp.sum(exchange(packet, CELL_AXIS), axis=0)
    center = arrived[:width] / total_cells
    twice_total = arrived[width : width + 2 * B][None]
    high, low = halves(arrived[width + 2 * B :][None])
    counted = jnp.concatenate([high] * 4 + [low] * 4, axis=0)

    centred = (partial - center[None]).reshape(n_z, n_core, own, width)
    kept = jnp.where(even, centred[:, 0], centred[:, 1])
    given = jnp.where(even, centred[:, 1], centred[:, 0]).astype(bf16)
    given, kept, twice_total, counted = together((given, kept, twice_total, counted))
    both = lax.all_gather(given, CORE_AXIS)
    taken = jnp.where(even, both[1], both[0])
    pairs = (kept + taken.astype(f32)).astype(bf16)
    embedding = jnp.sum(exchange(pairs, Z_AXIS).astype(f32), axis=0)
    own_rows = unit(embedding)
    unit_rows = gather(share(own_rows, Z_AXIS).reshape(n_z * own, width), CORE_AXIS)

    arrived = share(block_of(dot(assign, unit_rows), counted), Y_AXIS)
    sums = added(arrived[:, : 2 * mine]).astype(bf16)
    blocks = jnp.concatenate([sums, arrived[:, 2 * mine], arrived[:, 2 * mine + 4]], axis=0)
    blocks = share(blocks, X_AXIS)
    for _ in range(1, ITERS):
        weights, shares = local(
            partial_of(weights_kernel, total_cells),
            (jax.ShapeDtypeStruct((mine, group), f32), jax.ShapeDtypeStruct((1, group), f32)),
            blocks,
            twice_total,
            unit_rows,
            hot_four,
        )
        norm = jnp.sum(share(shares, GENE_AXIS), axis=0)
        block = local(
            sums_kernel,
            jax.ShapeDtypeStruct((2 * mine + mine // 2, 2 * B), bf16),
            weights,
            norm,
            unit_rows,
            hot_four,
        )
        blocks = everywhere(block)

    rows = local(
        partial_of(pack_kernel, total_cells),
        jax.ShapeDtypeStruct((mine, width + 2 * B), bf16),
        blocks,
        twice_total,
    )
    rows = gather(rows, GENE_AXIS)
    return finish(own_rows, own_twice, rows, embedding)


def solution(mesh):
    cells, genes = mesh.devices.shape
    mesh = jax.sharding.Mesh(
        mesh.devices.reshape(cells // X_SIZE, X_SIZE, genes // 2, 2),
        (Y_AXIS, X_AXIS, Z_AXIS, CORE_AXIS),
    )
    owners = P((Y_AXIS, X_AXIS, Z_AXIS, CORE_AXIS), None)
    placed = (P(CELL_AXIS, GENE_AXIS), owners, owners, P(GENE_AXIS, None))
    return jax.shard_map(
        per_device,
        mesh=mesh,
        in_specs=placed,
        out_specs=(owners, owners, P()),
        check_vma=False,
    )
```
